128 devices in a mesh: row: 8 (over x, z_lo), col: 16 (over z_hi, y, core).
Axes of the slice: x: 4, y: 4, z: 4 (z_hi: 2, z_lo: 2; z = z_hi * 2 + z_lo), core: 2. Of those that a mesh axis runs over, the one named last changes fastest.
Arguments:
- factor_tiles: float32 [16, 1024, 8, 2048], P(None, 'row', None, 'col'), may hold values from -40 to 40, as said below
Outputs:
- rotated: float32 [16384, 16384], P(None, ('row', 'col'))
The draws below stay inside these ranges and needn't reach their ends.
Inputs may be any that keep to these rules, and one draw needn't show every extreme that they name: `factor_tiles`: upper triangular: entries below the diagonal are zero, entries on it are positive.
All inputs are finite; a program needn't handle non-finite values.
Results may differ from the reference program's by a relative error of at most 0.0003.
Values sent between devices are 32-bit elements; how exact they have to be, the bound alone decides.
A program may use at most 128 MiB of HBM per device.

```python
import math
import jax
import jax.numpy as jnp
from jax import lax

LOGB = 7
OUTER = 4
INNER = 8
BLK = 128
NMAT = 16384
TILE_ROWS = 1024
TILE_COLS = 2048


def draw_factor_tiles(key, part):
    keys = jax.random.split(jax.random.fold_in(key, 11), 5)
    order = NMAT
    rough = jnp.clip(jax.random.normal(keys[0], (order, order), jnp.float32), -6.0, 6.0)
    common = jnp.clip(jax.random.normal(keys[1], (order, 1), jnp.float32), -4.0, 4.0)
    row_scale = jnp.exp(jax.random.uniform(keys[2], (order, 1), jnp.float32, math.log(0.5), math.log(2.0)))
    col_scale = jnp.exp(jax.random.uniform(keys[3], (1, order), jnp.float32, math.log(0.5), math.log(5.0)))
    leading = 0.5 + jax.random.uniform(keys[4], (1, order), jnp.float32)
    row_ids = jnp.arange(order)[:, None]
    col_ids = jnp.arange(order)[None, :]
    upper_part = (rough + common) * math.sqrt(2.0 / order)
    core = jnp.where(row_ids < col_ids, upper_part, jnp.where(row_ids == col_ids, leading, 0.0))
    full_matrix = row_scale * col_scale * core
    return full_matrix.reshape(order // TILE_ROWS, TILE_ROWS, order // TILE_COLS, TILE_COLS).astype(jnp.float32)


def setup_inputs(seed: int = 0) -> dict:
    splits = jax.random.split(jax.random.key(seed), 2)
    return {
        "factor_tiles": draw_factor_tiles(jax.random.fold_in(splits[1], 71), 0),
    }


damping_ratio = 0.01


def pair_turn(matrix_in, cosine, sine_val, stride):
    orig_shape = matrix_in.shape
    groups = orig_shape[-1] // (2 * stride)
    split_view = matrix_in.reshape(orig_shape[:-1] + (groups, 2, stride))
    lead_part = split_view[..., 0, :]
    tail_part = split_view[..., 1, :]
    combined = jnp.stack([cosine * lead_part - sine_val * tail_part, sine_val * lead_part + cosine * tail_part], axis=-2)
    return combined.reshape(orig_shape)


def pair_angles(gram_matrix, stride):
    lead_dims = gram_matrix.shape[:-2]
    order = gram_matrix.shape[-1]
    groups = order // (2 * stride)
    diagonal = jnp.diagonal(gram_matrix, axis1=-2, axis2=-1).reshape(lead_dims + (groups, 2, stride))
    diag_p = diagonal[..., 0, :]
    diag_q = diagonal[..., 1, :]
    pair_rows = gram_matrix.reshape(lead_dims + (groups, 2, stride, order))[..., 0, :, :]
    target = jnp.arange(groups)[:, None] * (2 * stride) + stride + jnp.arange(stride)[None, :]
    selector = jnp.arange(order)[None, None, :] == target[:, :, None]
    cross = jnp.sum(jnp.where(selector, pair_rows, 0.0), axis=-1)
    diag_gap = diag_q - diag_p
    diag_sum = diag_p + diag_q
    rot_angle = 0.5 * jnp.arctan2(2.0 * cross * diag_gap, diag_gap * diag_gap + damping_ratio * diag_sum * diag_sum)
    return jnp.cos(rot_angle), jnp.sin(rot_angle)


def inner_solve(gram_matrix):
    order = gram_matrix.shape[-1]
    accum = jnp.broadcast_to(jnp.eye(order, dtype=gram_matrix.dtype), gram_matrix.shape)
    for inner_step in range(INNER):
        bit_index = (LOGB - 1 - inner_step) % LOGB
        stride = 2 ** bit_index
        cosine, sine_val = pair_angles(gram_matrix, stride)
        cos_wide = cosine[..., None, :, :]
        sin_wide = sine_val[..., None, :, :]
        gram_matrix = pair_turn(gram_matrix, cos_wide, sin_wide, stride)
        gram_matrix = jnp.swapaxes(pair_turn(jnp.swapaxes(gram_matrix, -1, -2), cos_wide, sin_wide, stride), -1, -2)
        accum = pair_turn(accum, cos_wide, sin_wide, stride)
    return accum


def reference(factor_tiles):
    order = NMAT
    slots_total = order // BLK
    half_width = BLK // 2
    full_matrix = factor_tiles.reshape(order, order)
    slot_columns = jnp.transpose(full_matrix.reshape(order, slots_total, BLK), (1, 0, 2))
    for round_index in range(OUTER):
        gram_matrix = jnp.einsum("pni,pnj->pij", slot_columns, slot_columns, precision=lax.Precision.HIGHEST)
        rotation = inner_solve(gram_matrix)
        slot_columns = jnp.einsum("pni,pij->pnj", slot_columns, rotation, precision=lax.Precision.HIGHEST)
        if round_index + 1 < OUTER:
            top_half = slot_columns[:, :, :half_width]
            bottom_half = slot_columns[:, :, half_width:]
            outgoing = jnp.concatenate([bottom_half[:1], top_half[1:]], axis=0)
            new_top = jnp.concatenate([top_half[:1], outgoing[:-1]], axis=0)
            new_bottom = jnp.concatenate([bottom_half[1:], top_half[-1:]], axis=0)
            slot_columns = jnp.concatenate([new_top, new_bottom], axis=2)
    return jnp.transpose(slot_columns, (1, 0, 2)).reshape(order, order)
```

```python
import jax
import jax.numpy as jnp
from jax import lax
from jax.sharding import PartitionSpec as P

LOGB = 7
OUTER = 4
INNER = 8
CHUNKS = 4


damping_ratio = 0.01
highest = lax.Precision.HIGHEST


def passed_along(value, axis, steps):
    count = lax.axis_size(axis)
    leading, last = (max(0, -steps), min(count, count - steps))
    return lax.ppermute(value, axis, [(source, source + steps) for source in range(leading, last)])


def step_rotation(gram_matrix, stride):
    order = gram_matrix.shape[-1]
    index_row = jnp.arange(order)
    partner = jnp.bitwise_xor(index_row, stride)
    is_lead = jnp.bitwise_and(index_row, stride) == 0
    identity = index_row[:, None] == index_row[None, :]
    partner_mask = index_row[None, :] == partner[:, None]
    diagonal = jnp.sum(jnp.where(identity, gram_matrix, 0.0), axis=-1)
    diag_other = jnp.sum(jnp.where(partner_mask, diagonal[..., None, :], 0.0), axis=-1)
    cross_row = jnp.sum(jnp.where(partner_mask, gram_matrix, 0.0), axis=-1)
    cross_col = jnp.sum(jnp.where(partner_mask, gram_matrix, 0.0), axis=-2)
    diag_p = jnp.where(is_lead, diagonal, diag_other)
    diag_q = jnp.where(is_lead, diag_other, diagonal)
    cross = jnp.where(is_lead, cross_row, cross_col)
    diag_gap = diag_q - diag_p
    diag_sum = diag_p + diag_q
    rot_angle = 0.5 * jnp.arctan2(
        2.0 * cross * diag_gap, diag_gap * diag_gap + damping_ratio * diag_sum * diag_sum
    )
    cosine = jnp.cos(rot_angle)
    sine_val = jnp.where(is_lead, -jnp.sin(rot_angle), jnp.sin(rot_angle))
    turn = jnp.where(identity, cosine[..., None, :], 0.0)
    return turn + jnp.where(partner_mask, sine_val[..., None, :], 0.0)


def inner_solve(gram_matrix):
    order = gram_matrix.shape[-1]
    accum = jnp.eye(order, dtype=gram_matrix.dtype)
    for inner_step in range(INNER):
        bit_index = (LOGB - 1 - inner_step) % LOGB
        turn = step_rotation(gram_matrix, 2**bit_index)
        gram_matrix = jnp.einsum("...ik,...kj->...ij", gram_matrix, turn, precision=highest)
        gram_matrix = jnp.einsum("...ki,...kj->...ij", turn, gram_matrix, precision=highest)
        accum = jnp.einsum("...ik,...kj->...ij", accum, turn, precision=highest)
    return accum


def relayout(tile_work):
    cycles, row_count, tile_count, tile_width = tile_work.shape
    split_view = tile_work.reshape(cycles, 1, row_count, tile_count, tile_width)
    received = lax.all_to_all(split_view, "row", split_axis=3, concat_axis=1, tiled=True)
    return received.reshape(cycles * received.shape[1] * row_count, tile_width)


def summed(parts):
    total = parts[0]
    for part in parts[1:]:
        total = total + part
    return total


def per_device(factor_tiles):
    half_width = factor_tiles.shape[-1] // 2
    column_block = relayout(factor_tiles)
    rows = column_block.shape[0]
    span = rows // CHUNKS
    position = lax.axis_index(("row", "col"))
    devices_total = lax.axis_size(("row", "col"))
    first = position == 0
    last = position == devices_total - 1
    pieces = [column_block[j * span:(j + 1) * span] for j in range(CHUNKS)]
    gram_matrix = summed(
        [jnp.einsum("ni,nj->ij", piece, piece, precision=highest) for piece in pieces]
    )
    rotation = inner_solve(gram_matrix)
    lines = [jnp.einsum("ni,ij->jn", piece, rotation, precision=highest) for piece in pieces]
    for round_index in range(1, OUTER):
        fresh = []
        for piece in lines:
            top_half = piece[:half_width]
            bottom_half = piece[half_width:]
            outgoing = jnp.where(first, bottom_half, top_half)
            arrived = passed_along(outgoing, ("row", "col"), 1)
            behind = passed_along(bottom_half, ("row", "col"), -1)
            new_top = jnp.where(first, top_half, arrived)
            new_bottom = jnp.where(last, top_half, behind)
            fresh.append(jnp.concatenate([new_top, new_bottom], axis=0))
        gram_matrix = summed(
            [jnp.einsum("in,jn->ij", piece, piece, precision=highest) for piece in fresh]
        )
        rotation = inner_solve(gram_matrix)
        if round_index + 1 < OUTER:
            lines = [jnp.einsum("in,ij->jn", piece, rotation, precision=highest) for piece in fresh]
        else:
            return jnp.concatenate(
                [jnp.einsum("in,ij->nj", piece, rotation, precision=highest) for piece in fresh],
                axis=0,
            )


def solution(mesh):
    return jax.shard_map(
        per_device,
        mesh=mesh,
        in_specs=(P(None, "row", None, "col"),),
        out_specs=P(None, ("row", "col")),
        check_vma=False,
    )
```

```python
import jax
import jax.numpy as jnp
from jax import lax
from jax.sharding import PartitionSpec as P
from jax.experimental import pallas as pl
from jax.experimental.pallas import tpu as pltpu

MESH = pl.DeviceIdType.MESH

LOGB = 7
OUTER = 4
INNER = 8
CHUNKS = 4


damping_ratio = 0.01
highest = lax.Precision.HIGHEST


def passed_along(value, axis, steps):
    count = lax.axis_size(axis)
    leading, last = (max(0, -steps), min(count, count - steps))
    return lax.ppermute(value, axis, [(source, source + steps) for source in range(leading, last)])


def step_rotation(gram_matrix, stride):
    order = gram_matrix.shape[-1]
    index_row = jnp.arange(order)
    partner = jnp.bitwise_xor(index_row, stride)
    is_lead = jnp.bitwise_and(index_row, stride) == 0
    identity = index_row[:, None] == index_row[None, :]
    partner_mask = index_row[None, :] == partner[:, None]
    diagonal = jnp.sum(jnp.where(identity, gram_matrix, 0.0), axis=-1)
    diag_other = jnp.sum(jnp.where(partner_mask, diagonal[..., None, :], 0.0), axis=-1)
    cross_row = jnp.sum(jnp.where(partner_mask, gram_matrix, 0.0), axis=-1)
    cross_col = jnp.sum(jnp.where(partner_mask, gram_matrix, 0.0), axis=-2)
    diag_p = jnp.where(is_lead, diagonal, diag_other)
    diag_q = jnp.where(is_lead, diag_other, diagonal)
    cross = jnp.where(is_lead, cross_row, cross_col)
    diag_gap = diag_q - diag_p
    diag_sum = diag_p + diag_q
    rot_angle = 0.5 * jnp.arctan2(
        2.0 * cross * diag_gap, diag_gap * diag_gap + damping_ratio * diag_sum * diag_sum
    )
    cosine = jnp.cos(rot_angle)
    sine_val = jnp.where(is_lead, -jnp.sin(rot_angle), jnp.sin(rot_angle))
    turn = jnp.where(identity, cosine[..., None, :], 0.0)
    return turn + jnp.where(partner_mask, sine_val[..., None, :], 0.0)


def inner_solve(gram_matrix):
    order = gram_matrix.shape[-1]
    accum = jnp.eye(order, dtype=gram_matrix.dtype)
    for inner_step in range(INNER):
        bit_index = (LOGB - 1 - inner_step) % LOGB
        turn = step_rotation(gram_matrix, 2**bit_index)
        gram_matrix = jnp.einsum("...ik,...kj->...ij", gram_matrix, turn, precision=highest)
        gram_matrix = jnp.einsum("...ki,...kj->...ij", turn, gram_matrix, precision=highest)
        accum = jnp.einsum("...ik,...kj->...ij", accum, turn, precision=highest)
    return accum


def relayout(tile_work):
    cycles, row_count, tile_count, tile_width = tile_work.shape
    split_view = tile_work.reshape(cycles, 1, row_count, tile_count, tile_width)
    received = lax.all_to_all(split_view, "row", split_axis=3, concat_axis=1, tiled=True)
    return received.reshape(cycles * received.shape[1] * row_count, tile_width)


def gather_kernel(src_ref, zero_ref, out_ref, send_sem, recv_sem, local_sem):
    del zero_ref
    tiles, cycles, height, width = src_ref.shape
    me_r = lax.axis_index("row")
    me_c = lax.axis_index("col")
    n_c = lax.axis_size("col")
    k_me = me_r * n_c + me_c

    barrier = pltpu.get_barrier_semaphore()
    for t in range(tiles):
        @pl.when(me_r != t)
        def _():
            pl.semaphore_signal(barrier, inc=1, device_id=(t, me_c), device_id_type=MESH)
    pl.semaphore_wait(barrier, tiles - 1)

    def rows_of(block):
        return out_ref.at[pl.ds(pl.multiple_of(block * height, height), height)]

    sends = []
    locals_ = []
    for i in range(cycles):
        block = i * tiles + me_r
        local = pltpu.make_async_copy(src_ref.at[me_r, i], rows_of(block), local_sem.at[i])
        pl.when(block <= k_me)(local.start)
        locals_.append((block <= k_me, local))
        for t in range(tiles):
            wanted = (block <= t * n_c + me_c) & (me_r != t)
            copy = pltpu.make_async_remote_copy(
                src_ref=src_ref.at[t, i],
                dst_ref=rows_of(block),
                send_sem=send_sem.at[t, i],
                recv_sem=recv_sem.at[me_r, i],
                device_id=(t, me_c),
                device_id_type=MESH,
            )
            pl.when(wanted)(copy.start)
            sends.append((wanted, copy))
    for i in range(cycles):
        for r in range(tiles):
            block = i * tiles + r
            wanted = (block <= k_me) & (me_r != r)
            incoming = pltpu.make_async_remote_copy(
                src_ref=src_ref.at[r, i],
                dst_ref=rows_of(block),
                send_sem=send_sem.at[r, i],
                recv_sem=recv_sem.at[r, i],
                device_id=(r, me_c),
                device_id_type=MESH,
            )
            pl.when(wanted)(incoming.wait_recv)
    for wanted, copy in sends:
        pl.when(wanted)(copy.wait_send)
    for wanted, copy in locals_:
        pl.when(wanted)(copy.wait)


def gather_columns(factor_tiles):
    cycles, height, tiles, width = factor_tiles.shape
    by_tile = jnp.transpose(factor_tiles, (2, 0, 1, 3))
    zeros = jnp.zeros((cycles * tiles * height, width), factor_tiles.dtype)
    return pl.pallas_call(
        gather_kernel,
        out_shape=jax.ShapeDtypeStruct(zeros.shape, zeros.dtype),
        in_specs=[pl.BlockSpec(memory_space=pl.ANY)] * 2,
        out_specs=pl.BlockSpec(memory_space=pl.ANY),
        scratch_shapes=[
            pltpu.SemaphoreType.DMA((tiles, cycles)),
            pltpu.SemaphoreType.DMA((tiles, cycles)),
            pltpu.SemaphoreType.DMA((cycles,)),
        ],
        input_output_aliases={1: 0},
        compiler_params=pltpu.CompilerParams(collective_id=0, has_side_effects=True),
    )(by_tile, zeros)


def summed(parts):
    total = parts[0]
    for part in parts[1:]:
        total = total + part
    return total


def per_device(factor_tiles):
    half_width = factor_tiles.shape[-1] // 2
    column_block = gather_columns(factor_tiles)
    rows = column_block.shape[0]
    span = rows // CHUNKS
    position = lax.axis_index(("row", "col"))
    devices_total = lax.axis_size(("row", "col"))
    first = position == 0
    last = position == devices_total - 1
    pieces = [column_block[j * span:(j + 1) * span] for j in range(CHUNKS)]
    gram_matrix = summed(
        [jnp.einsum("ni,nj->ij", piece, piece, precision=highest) for piece in pieces]
    )
    rotation = inner_solve(gram_matrix)
    lines = [jnp.einsum("ni,ij->jn", piece, rotation, precision=highest) for piece in pieces]
    for round_index in range(1, OUTER):
        fresh = []
        for piece in lines:
            top_half = piece[:half_width]
            bottom_half = piece[half_width:]
            outgoing = jnp.where(first, bottom_half, top_half)
            arrived = passed_along(outgoing, ("row", "col"), 1)
            behind = passed_along(bottom_half, ("row", "col"), -1)
            new_top = jnp.where(first, top_half, arrived)
            new_bottom = jnp.where(last, top_half, behind)
            fresh.append(jnp.concatenate([new_top, new_bottom], axis=0))
        gram_matrix = summed(
            [jnp.einsum("in,jn->ij", piece, piece, precision=highest) for piece in fresh]
        )
        rotation = inner_solve(gram_matrix)
        if round_index + 1 < OUTER:
            lines = [jnp.einsum("in,ij->jn", piece, rotation, precision=highest) for piece in fresh]
        else:
            whole = jnp.concatenate(fresh, axis=1)
            return jnp.einsum("in,ij->nj", whole, rotation, precision=highest)


def solution(mesh):
    return jax.shard_map(
        per_device,
        mesh=mesh,
        in_specs=(P(None, "row", None, "col"),),
        out_specs=P(None, ("row", "col")),
        check_vma=False,
    )
```

```python
import jax
import jax.numpy as jnp
from jax import lax
from jax.sharding import PartitionSpec as P
from jax.experimental import pallas as pl
from jax.experimental.pallas import tpu as pltpu

MESH = pl.DeviceIdType.MESH

LOGB = 7
OUTER = 4
INNER = 8
CHUNKS = 4


damping_ratio = 0.01
highest = lax.Precision.HIGHEST


def passed_along(value, axis, steps):
    count = lax.axis_size(axis)
    leading, last = (max(0, -steps), min(count, count - steps))
    return lax.ppermute(value, axis, [(source, source + steps) for source in range(leading, last)])


def solve_kernel(g_ref, q_ref):
    order = g_ref.shape[0]
    gram_matrix = g_ref[...]
    rows = lax.broadcasted_iota(jnp.int32, (order, order), 0)
    cols = lax.broadcasted_iota(jnp.int32, (order, order), 1)
    identity = rows == cols
    accum = jnp.where(identity, 1.0, 0.0).astype(gram_matrix.dtype)
    lane_ids = lax.broadcasted_iota(jnp.int32, (8, order), 1)
    for inner_step in range(INNER):
        stride = 2 ** ((LOGB - 1 - inner_step) % LOGB)

        def lane_partner(value):
            lead = (lax.broadcasted_iota(jnp.int32, value.shape, 1) & stride) == 0
            ahead = pltpu.roll(value, order - stride, 1)
            behind = pltpu.roll(value, stride, 1)
            return jnp.where(lead, ahead, behind)

        def row_partner(value):
            lead = (lax.broadcasted_iota(jnp.int32, value.shape, 0) & stride) == 0
            ahead = pltpu.roll(value, order - stride, 0)
            behind = pltpu.roll(value, stride, 0)
            return jnp.where(lead, ahead, behind)

        lane_lead = (lane_ids & stride) == 0
        diagonal = jnp.broadcast_to(
            jnp.sum(jnp.where(identity, gram_matrix, 0.0), axis=0, keepdims=True), (8, order)
        )
        cross_tail = jnp.broadcast_to(
            jnp.sum(jnp.where(rows == (cols ^ stride), gram_matrix, 0.0), axis=0, keepdims=True),
            (8, order),
        )
        diag_other = lane_partner(diagonal)
        diag_p = jnp.where(lane_lead, diagonal, diag_other)
        diag_q = jnp.where(lane_lead, diag_other, diagonal)
        cross = jnp.where(lane_lead, lane_partner(cross_tail), cross_tail)
        diag_gap = diag_q - diag_p
        diag_sum = diag_p + diag_q
        rot_angle = 0.5 * jnp.arctan2(
            2.0 * cross * diag_gap, diag_gap * diag_gap + damping_ratio * diag_sum * diag_sum
        )
        cosine = jnp.cos(rot_angle)
        sine_val = jnp.sin(rot_angle)
        signed_sine = jnp.where(lane_lead, -sine_val, sine_val)
        cos_lane = jnp.broadcast_to(cosine[:1], (order, order))
        sin_lane = jnp.broadcast_to(signed_sine[:1], (order, order))
        cos_row = jnp.sum(jnp.where(identity, cos_lane, 0.0), axis=1, keepdims=True)
        sin_row = jnp.sum(jnp.where(identity, sin_lane, 0.0), axis=1, keepdims=True)
        gram_matrix = cos_lane * gram_matrix + sin_lane * lane_partner(gram_matrix)
        gram_matrix = cos_row * gram_matrix + sin_row * row_partner(gram_matrix)
        accum = cos_lane * accum + sin_lane * lane_partner(accum)
    q_ref[...] = accum


def inner_solve(gram_matrix):
    return pl.pallas_call(
        solve_kernel,
        out_shape=jax.ShapeDtypeStruct(gram_matrix.shape, gram_matrix.dtype),
    )(gram_matrix)


def relayout(tile_work):
    cycles, row_count, tile_count, tile_width = tile_work.shape
    split_view = tile_work.reshape(cycles, 1, row_count, tile_count, tile_width)
    received = lax.all_to_all(split_view, "row", split_axis=3, concat_axis=1, tiled=True)
    return received.reshape(cycles * received.shape[1] * row_count, tile_width)


def gather_kernel(src_ref, zero_ref, out_ref, send_sem, recv_sem, local_sem):
    del zero_ref
    tiles, cycles, height, width = src_ref.shape
    me_r = lax.axis_index("row")
    me_c = lax.axis_index("col")
    n_c = lax.axis_size("col")
    k_me = me_r * n_c + me_c

    barrier = pltpu.get_barrier_semaphore()
    for t in range(tiles):
        @pl.when(me_r != t)
        def _():
            pl.semaphore_signal(barrier, inc=1, device_id=(t, me_c), device_id_type=MESH)
    pl.semaphore_wait(barrier, tiles - 1)

    def rows_of(block):
        return out_ref.at[pl.ds(pl.multiple_of(block * height, height), height)]

    sends = []
    locals_ = []
    for i in range(cycles):
        block = i * tiles + me_r
        local = pltpu.make_async_copy(src_ref.at[me_r, i], rows_of(block), local_sem.at[i])
        pl.when(block <= k_me)(local.start)
        locals_.append((block <= k_me, local))
        for t in range(tiles):
            wanted = (block <= t * n_c + me_c) & (me_r != t)
            copy = pltpu.make_async_remote_copy(
                src_ref=src_ref.at[t, i],
                dst_ref=rows_of(block),
                send_sem=send_sem.at[t, i],
                recv_sem=recv_sem.at[me_r, i],
                device_id=(t, me_c),
                device_id_type=MESH,
            )
            pl.when(wanted)(copy.start)
            sends.append((wanted, copy))
    for i in range(cycles):
        for r in range(tiles):
            block = i * tiles + r
            wanted = (block <= k_me) & (me_r != r)
            incoming = pltpu.make_async_remote_copy(
                src_ref=src_ref.at[r, i],
                dst_ref=rows_of(block),
                send_sem=send_sem.at[r, i],
                recv_sem=recv_sem.at[r, i],
                device_id=(r, me_c),
                device_id_type=MESH,
            )
            pl.when(wanted)(incoming.wait_recv)
    for wanted, copy in sends:
        pl.when(wanted)(copy.wait_send)
    for wanted, copy in locals_:
        pl.when(wanted)(copy.wait)


def gather_columns(factor_tiles):
    cycles, height, tiles, width = factor_tiles.shape
    by_tile = jnp.transpose(factor_tiles, (2, 0, 1, 3))
    zeros = jnp.zeros((cycles * tiles * height, width), factor_tiles.dtype)
    return pl.pallas_call(
        gather_kernel,
        out_shape=jax.ShapeDtypeStruct(zeros.shape, zeros.dtype),
        in_specs=[pl.BlockSpec(memory_space=pl.ANY)] * 2,
        out_specs=pl.BlockSpec(memory_space=pl.ANY),
        scratch_shapes=[
            pltpu.SemaphoreType.DMA((tiles, cycles)),
            pltpu.SemaphoreType.DMA((tiles, cycles)),
            pltpu.SemaphoreType.DMA((cycles,)),
        ],
        input_output_aliases={1: 0},
        compiler_params=pltpu.CompilerParams(collective_id=0, has_side_effects=True),
    )(by_tile, zeros)


def summed(parts):
    total = parts[0]
    for part in parts[1:]:
        total = total + part
    return total


def per_device(factor_tiles):
    half_width = factor_tiles.shape[-1] // 2
    column_block = gather_columns(factor_tiles)
    rows = column_block.shape[0]
    span = rows // CHUNKS
    position = lax.axis_index(("row", "col"))
    devices_total = lax.axis_size(("row", "col"))
    first = position == 0
    last = position == devices_total - 1
    pieces = [column_block[j * span:(j + 1) * span] for j in range(CHUNKS)]
    gram_matrix = summed(
        [jnp.einsum("ni,nj->ij", piece, piece, precision=highest) for piece in pieces]
    )
    rotation = inner_solve(gram_matrix)
    lines = [jnp.einsum("ni,ij->jn", piece, rotation, precision=highest) for piece in pieces]
    for round_index in range(1, OUTER):
        fresh = []
        for piece in lines:
            top_half = piece[:half_width]
            bottom_half = piece[half_width:]
            outgoing = jnp.where(first, bottom_half, top_half)
            arrived = passed_along(outgoing, ("row", "col"), 1)
            behind = passed_along(bottom_half, ("row", "col"), -1)
            new_top = jnp.where(first, top_half, arrived)
            new_bottom = jnp.where(last, top_half, behind)
            fresh.append(jnp.concatenate([new_top, new_bottom], axis=0))
        gram_matrix = summed(
            [jnp.einsum("in,jn->ij", piece, piece, precision=highest) for piece in fresh]
        )
        rotation = inner_solve(gram_matrix)
        if round_index + 1 < OUTER:
            lines = [jnp.einsum("in,ij->jn", piece, rotation, precision=highest) for piece in fresh]
        else:
            whole = jnp.concatenate(fresh, axis=1)
            return jnp.einsum("in,ij->nj", whole, rotation, precision=highest)


def solution(mesh):
    return jax.shard_map(
        per_device,
        mesh=mesh,
        in_specs=(P(None, "row", None, "col"),),
        out_specs=P(None, ("row", "col")),
        check_vma=False,
    )
```

```python
import jax
import jax.numpy as jnp
from jax import lax
from jax.sharding import PartitionSpec as P
from jax.experimental import pallas as pl
from jax.experimental.pallas import tpu as pltpu

MESH = pl.DeviceIdType.MESH

LOGB = 7
OUTER = 4
INNER = 8
CHUNKS = 4


damping_ratio = 0.01
highest = lax.Precision.HIGHEST


def passed_along(value, axis, steps):
    count = lax.axis_size(axis)
    leading, last = (max(0, -steps), min(count, count - steps))
    return lax.ppermute(value, axis, [(source, source + steps) for source in range(leading, last)])


def solve_kernel(g_ref, q_ref):
    order = g_ref.shape[0]
    gram_matrix = g_ref[...]
    rows = lax.broadcasted_iota(jnp.int32, (order, order), 0)
    cols = lax.broadcasted_iota(jnp.int32, (order, order), 1)
    identity = rows == cols
    accum = jnp.where(identity, 1.0, 0.0).astype(gram_matrix.dtype)
    lane_ids = lax.broadcasted_iota(jnp.int32, (8, order), 1)
    for inner_step in range(INNER):
        stride = 2 ** ((LOGB - 1 - inner_step) % LOGB)

        def lane_partner(value):
            lead = (lax.broadcasted_iota(jnp.int32, value.shape, 1) & stride) == 0
            ahead = pltpu.roll(value, order - stride, 1)
            behind = pltpu.roll(value, stride, 1)
            return jnp.where(lead, ahead, behind)

        def row_partner(value):
            lead = (lax.broadcasted_iota(jnp.int32, value.shape, 0) & stride) == 0
            ahead = pltpu.roll(value, order - stride, 0)
            behind = pltpu.roll(value, stride, 0)
            return jnp.where(lead, ahead, behind)

        lane_lead = (lane_ids & stride) == 0
        diagonal = jnp.broadcast_to(
            jnp.sum(jnp.where(identity, gram_matrix, 0.0), axis=0, keepdims=True), (8, order)
        )
        cross_tail = jnp.broadcast_to(
            jnp.sum(jnp.where(rows == (cols ^ stride), gram_matrix, 0.0), axis=0, keepdims=True),
            (8, order),
        )
        diag_other = lane_partner(diagonal)
        diag_p = jnp.where(lane_lead, diagonal, diag_other)
        diag_q = jnp.where(lane_lead, diag_other, diagonal)
        cross = jnp.where(lane_lead, lane_partner(cross_tail), cross_tail)
        diag_gap = diag_q - diag_p
        diag_sum = diag_p + diag_q
        rot_angle = 0.5 * jnp.arctan2(
            2.0 * cross * diag_gap, diag_gap * diag_gap + damping_ratio * diag_sum * diag_sum
        )
        cosine = jnp.cos(rot_angle)
        sine_val = jnp.sin(rot_angle)
        signed_sine = jnp.where(lane_lead, -sine_val, sine_val)
        cos_lane = jnp.broadcast_to(cosine[:1], (order, order))
        sin_lane = jnp.broadcast_to(signed_sine[:1], (order, order))
        cos_row = jnp.sum(jnp.where(identity, cos_lane, 0.0), axis=1, keepdims=True)
        sin_row = jnp.sum(jnp.where(identity, sin_lane, 0.0), axis=1, keepdims=True)
        gram_matrix = cos_lane * gram_matrix + sin_lane * lane_partner(gram_matrix)
        gram_matrix = cos_row * gram_matrix + sin_row * row_partner(gram_matrix)
        accum = cos_lane * accum + sin_lane * lane_partner(accum)
    q_ref[...] = accum


def inner_solve(gram_matrix):
    return pl.pallas_call(
        solve_kernel,
        out_shape=jax.ShapeDtypeStruct(gram_matrix.shape, gram_matrix.dtype),
    )(gram_matrix)


def relayout(tile_work):
    cycles, row_count, tile_count, tile_width = tile_work.shape
    split_view = tile_work.reshape(cycles, 1, row_count, tile_count, tile_width)
    received = lax.all_to_all(split_view, "row", split_axis=3, concat_axis=1, tiled=True)
    return received.reshape(cycles * received.shape[1] * row_count, tile_width)


def gather_kernel(src_ref, out_ref, zero_buf, send_sem, recv_sem, local_sem, zero_sem):
    cycles, height, tiles, width = src_ref.shape
    me_r = lax.axis_index("row")
    me_c = lax.axis_index("col")
    n_c = lax.axis_size("col")
    k_me = me_r * n_c + me_c

    barrier = pltpu.get_barrier_semaphore()
    for t in range(tiles):
        @pl.when(me_r != t)
        def _():
            pl.semaphore_signal(barrier, inc=1, device_id=(t, me_c), device_id_type=MESH)
    pl.semaphore_wait(barrier, tiles - 1)

    def rows_of(block):
        return out_ref.at[pl.ds(pl.multiple_of(block * height, height), height)]

    sends = []
    locals_ = []
    for i in range(cycles):
        block = i * tiles + me_r
        local = pltpu.make_async_copy(src_ref.at[i, :, me_r, :], rows_of(block), local_sem.at[i])
        pl.when(block <= k_me)(local.start)
        locals_.append((block <= k_me, local))
        for t in range(tiles):
            wanted = (block <= t * n_c + me_c) & (me_r != t)
            copy = pltpu.make_async_remote_copy(
                src_ref=src_ref.at[i, :, t, :],
                dst_ref=rows_of(block),
                send_sem=send_sem.at[t, i],
                recv_sem=recv_sem.at[me_r, i],
                device_id=(t, me_c),
                device_id_type=MESH,
            )
            pl.when(wanted)(copy.start)
            sends.append((wanted, copy))
    zero_buf[...] = jnp.zeros_like(zero_buf)
    zeros = []
    for i in range(cycles):
        for r in range(tiles):
            block = i * tiles + r
            fill = pltpu.make_async_copy(zero_buf, rows_of(block), zero_sem.at[r, i])
            pl.when(block > k_me)(fill.start)
            zeros.append((block > k_me, fill))
    for i in range(cycles):
        for r in range(tiles):
            block = i * tiles + r
            wanted = (block <= k_me) & (me_r != r)
            incoming = pltpu.make_async_remote_copy(
                src_ref=src_ref.at[i, :, r, :],
                dst_ref=rows_of(block),
                send_sem=send_sem.at[r, i],
                recv_sem=recv_sem.at[r, i],
                device_id=(r, me_c),
                device_id_type=MESH,
            )
            pl.when(wanted)(incoming.wait_recv)
    for wanted, copy in sends:
        pl.when(wanted)(copy.wait_send)
    for wanted, copy in locals_ + zeros:
        pl.when(wanted)(copy.wait)


def gather_columns(factor_tiles):
    cycles, height, tiles, width = factor_tiles.shape
    return pl.pallas_call(
        gather_kernel,
        out_shape=jax.ShapeDtypeStruct((cycles * tiles * height, width), factor_tiles.dtype),
        in_specs=[pl.BlockSpec(memory_space=pl.ANY)],
        out_specs=pl.BlockSpec(memory_space=pl.ANY),
        scratch_shapes=[
            pltpu.VMEM((height, width), factor_tiles.dtype),
            pltpu.SemaphoreType.DMA((tiles, cycles)),
            pltpu.SemaphoreType.DMA((tiles, cycles)),
            pltpu.SemaphoreType.DMA((cycles,)),
            pltpu.SemaphoreType.DMA((tiles, cycles)),
        ],
        compiler_params=pltpu.CompilerParams(collective_id=0, has_side_effects=True),
    )(factor_tiles)


def summed(parts):
    total = parts[0]
    for part in parts[1:]:
        total = total + part
    return total


def per_device(factor_tiles):
    half_width = factor_tiles.shape[-1] // 2
    column_block = gather_columns(factor_tiles)
    rows = column_block.shape[0]
    span = rows // CHUNKS
    position = lax.axis_index(("row", "col"))
    devices_total = lax.axis_size(("row", "col"))
    first = position == 0
    last = position == devices_total - 1
    pieces = [column_block[j * span:(j + 1) * span] for j in range(CHUNKS)]
    gram_matrix = jnp.einsum("ni,nj->ij", column_block, column_block, precision=highest)
    rotation = inner_solve(gram_matrix)
    lines = [jnp.einsum("ni,ij->jn", piece, rotation, precision=highest) for piece in pieces]
    for round_index in range(1, OUTER):
        fresh = []
        for piece in lines:
            top_half = piece[:half_width]
            bottom_half = piece[half_width:]
            outgoing = jnp.where(first, bottom_half, top_half)
            arrived = passed_along(outgoing, ("row", "col"), 1)
            behind = passed_along(bottom_half, ("row", "col"), -1)
            new_top = jnp.where(first, top_half, arrived)
            new_bottom = jnp.where(last, top_half, behind)
            fresh.append(jnp.concatenate([new_top, new_bottom], axis=0))
        gram_matrix = summed(
            [jnp.einsum("in,jn->ij", piece, piece, precision=highest) for piece in fresh]
        )
        rotation = inner_solve(gram_matrix)
        if round_index + 1 < OUTER:
            lines = [jnp.einsum("in,ij->jn", piece, rotation, precision=highest) for piece in fresh]
        else:
            whole = jnp.concatenate(fresh, axis=1)
            return jnp.einsum("in,ij->nj", whole, rotation, precision=highest)


def solution(mesh):
    return jax.shard_map(
        per_device,
        mesh=mesh,
        in_specs=(P(None, "row", None, "col"),),
        out_specs=P(None, ("row", "col")),
        check_vma=False,
    )
```

```python
import jax
import jax.numpy as jnp
from jax import lax
from jax.sharding import PartitionSpec as P
from jax.experimental import pallas as pl
from jax.experimental.pallas import tpu as pltpu

MESH = pl.DeviceIdType.MESH

LOGB = 7
OUTER = 4
INNER = 8
CHUNKS = 4


damping_ratio = 0.01
highest = lax.Precision.HIGHEST


def passed_along(value, axis, steps):
    count = lax.axis_size(axis)
    leading, last = (max(0, -steps), min(count, count - steps))
    return lax.ppermute(value, axis, [(source, source + steps) for source in range(leading, last)])


def solve_kernel(g_ref, q_ref):
    order = g_ref.shape[0]
    gram_matrix = g_ref[...]
    rows = lax.broadcasted_iota(jnp.int32, (order, order), 0)
    cols = lax.broadcasted_iota(jnp.int32, (order, order), 1)
    identity = rows == cols
    accum = jnp.where(identity, 1.0, 0.0).astype(gram_matrix.dtype)
    lane_ids = lax.broadcasted_iota(jnp.int32, (8, order), 1)
    for inner_step in range(INNER):
        stride = 2 ** ((LOGB - 1 - inner_step) % LOGB)

        def lane_partner(value):
            lead = (lax.broadcasted_iota(jnp.int32, value.shape, 1) & stride) == 0
            ahead = pltpu.roll(value, order - stride, 1)
            behind = pltpu.roll(value, stride, 1)
            return jnp.where(lead, ahead, behind)

        def row_partner(value):
            lead = (lax.broadcasted_iota(jnp.int32, value.shape, 0) & stride) == 0
            ahead = pltpu.roll(value, order - stride, 0)
            behind = pltpu.roll(value, stride, 0)
            return jnp.where(lead, ahead, behind)

        lane_lead = (lane_ids & stride) == 0
        diagonal = jnp.broadcast_to(
            jnp.sum(jnp.where(identity, gram_matrix, 0.0), axis=0, keepdims=True), (8, order)
        )
        cross_tail = jnp.broadcast_to(
            jnp.sum(jnp.where(rows == (cols ^ stride), gram_matrix, 0.0), axis=0, keepdims=True),
            (8, order),
        )
        diag_other = lane_partner(diagonal)
        diag_p = jnp.where(lane_lead, diagonal, diag_other)
        diag_q = jnp.where(lane_lead, diag_other, diagonal)
        cross = jnp.where(lane_lead, lane_partner(cross_tail), cross_tail)
        diag_gap = diag_q - diag_p
        diag_sum = diag_p + diag_q
        rot_angle = 0.5 * jnp.arctan2(
            2.0 * cross * diag_gap, diag_gap * diag_gap + damping_ratio * diag_sum * diag_sum
        )
        cosine = jnp.cos(rot_angle)
        sine_val = jnp.sin(rot_angle)
        signed_sine = jnp.where(lane_lead, -sine_val, sine_val)
        cos_lane = jnp.broadcast_to(cosine[:1], (order, order))
        sin_lane = jnp.broadcast_to(signed_sine[:1], (order, order))
        cos_row = jnp.sum(jnp.where(identity, cos_lane, 0.0), axis=1, keepdims=True)
        sin_row = jnp.sum(jnp.where(identity, sin_lane, 0.0), axis=1, keepdims=True)
        gram_matrix = cos_lane * gram_matrix + sin_lane * lane_partner(gram_matrix)
        gram_matrix = cos_row * gram_matrix + sin_row * row_partner(gram_matrix)
        accum = cos_lane * accum + sin_lane * lane_partner(accum)
    q_ref[...] = accum


def inner_solve(gram_matrix):
    return pl.pallas_call(
        solve_kernel,
        out_shape=jax.ShapeDtypeStruct(gram_matrix.shape, gram_matrix.dtype),
    )(gram_matrix)


def relayout(tile_work):
    cycles, row_count, tile_count, tile_width = tile_work.shape
    split_view = tile_work.reshape(cycles, 1, row_count, tile_count, tile_width)
    received = lax.all_to_all(split_view, "row", split_axis=3, concat_axis=1, tiled=True)
    return received.reshape(cycles * received.shape[1] * row_count, tile_width)


def gather_kernel(src_ref, out_ref, zero_buf, send_sem, recv_sem, local_sem, zero_sem):
    cycles, height, tiles, width = src_ref.shape
    me_r = lax.axis_index("row")
    me_c = lax.axis_index("col")
    n_c = lax.axis_size("col")
    k_me = me_r * n_c + me_c

    barrier = pltpu.get_barrier_semaphore()
    for t in range(tiles):
        @pl.when(me_r != t)
        def _():
            pl.semaphore_signal(barrier, inc=1, device_id=(t, me_c), device_id_type=MESH)
    pl.semaphore_wait(barrier, tiles - 1)

    def rows_of(block):
        return out_ref.at[pl.ds(pl.multiple_of(block * height, height), height)]

    sends = []
    locals_ = []
    for i in range(cycles):
        block = i * tiles + me_r
        local = pltpu.make_async_copy(src_ref.at[i, :, me_r, :], rows_of(block), local_sem.at[i])
        pl.when(block <= k_me)(local.start)
        locals_.append((block <= k_me, local))
        for t in range(tiles):
            wanted = (block <= t * n_c + me_c) & (me_r != t)
            copy = pltpu.make_async_remote_copy(
                src_ref=src_ref.at[i, :, t, :],
                dst_ref=rows_of(block),
                send_sem=send_sem.at[t, i],
                recv_sem=recv_sem.at[me_r, i],
                device_id=(t, me_c),
                device_id_type=MESH,
            )
            pl.when(wanted)(copy.start)
            sends.append((wanted, copy))
    zero_buf[...] = jnp.zeros_like(zero_buf)
    zeros = []
    for i in range(cycles):
        for r in range(tiles):
            block = i * tiles + r
            fill = pltpu.make_async_copy(zero_buf, rows_of(block), zero_sem.at[r, i])
            pl.when(block > k_me)(fill.start)
            zeros.append((block > k_me, fill))
    for i in range(cycles):
        for r in range(tiles):
            block = i * tiles + r
            wanted = (block <= k_me) & (me_r != r)
            incoming = pltpu.make_async_remote_copy(
                src_ref=src_ref.at[i, :, r, :],
                dst_ref=rows_of(block),
                send_sem=send_sem.at[r, i],
                recv_sem=recv_sem.at[r, i],
                device_id=(r, me_c),
                device_id_type=MESH,
            )
            pl.when(wanted)(incoming.wait_recv)
    for wanted, copy in sends:
        pl.when(wanted)(copy.wait_send)
    for wanted, copy in locals_ + zeros:
        pl.when(wanted)(copy.wait)


def gather_columns(factor_tiles):
    cycles, height, tiles, width = factor_tiles.shape
    return pl.pallas_call(
        gather_kernel,
        out_shape=jax.ShapeDtypeStruct((cycles * tiles * height, width), factor_tiles.dtype),
        in_specs=[pl.BlockSpec(memory_space=pl.ANY)],
        out_specs=pl.BlockSpec(memory_space=pl.ANY),
        scratch_shapes=[
            pltpu.VMEM((height, width), factor_tiles.dtype),
            pltpu.SemaphoreType.DMA((tiles, cycles)),
            pltpu.SemaphoreType.DMA((tiles, cycles)),
            pltpu.SemaphoreType.DMA((cycles,)),
            pltpu.SemaphoreType.DMA((tiles, cycles)),
        ],
        compiler_params=pltpu.CompilerParams(collective_id=0, has_side_effects=True),
    )(factor_tiles)


def exchange_kernel(lines_ref, new_ref, send_sem, recv_sem):
    order, width = lines_ref.shape
    half = order // 2
    span = width // CHUNKS
    n_c = lax.axis_size("col")
    total = lax.axis_size("row") * n_c
    me = lax.axis_index("row") * n_c + lax.axis_index("col")
    has_left = me > 0
    has_right = me < total - 1
    left = jnp.maximum(me - 1, 0)
    right = jnp.minimum(me + 1, total - 1)
    left_id = (left // n_c, left % n_c)
    right_id = (right // n_c, right % n_c)

    barrier = pltpu.get_barrier_semaphore()

    @pl.when(has_left)
    def _():
        pl.semaphore_signal(barrier, inc=1, device_id=left_id, device_id_type=MESH)

    @pl.when(has_right)
    def _():
        pl.semaphore_signal(barrier, inc=1, device_id=right_id, device_id_type=MESH)

    pl.semaphore_wait(barrier, has_left.astype(jnp.int32) + has_right.astype(jnp.int32))

    first_row = jnp.where(me == 0, half, 0)
    copies = []
    for j in range(CHUNKS):
        cols = pl.ds(j * span, span)
        to_right = pltpu.make_async_remote_copy(
            src_ref=lines_ref.at[pl.ds(pl.multiple_of(first_row, half), half), cols],
            dst_ref=new_ref.at[pl.ds(0, half), cols],
            send_sem=send_sem.at[0, j],
            recv_sem=recv_sem.at[0, j],
            device_id=right_id,
            device_id_type=MESH,
        )
        to_left = pltpu.make_async_remote_copy(
            src_ref=lines_ref.at[pl.ds(half, half), cols],
            dst_ref=new_ref.at[pl.ds(half, half), cols],
            send_sem=send_sem.at[1, j],
            recv_sem=recv_sem.at[1, j],
            device_id=left_id,
            device_id_type=MESH,
        )
        pl.when(has_right)(to_right.start)
        pl.when(has_left)(to_left.start)
        copies.append((to_right, to_left))
    for to_right, to_left in copies:
        pl.when(has_left)(to_right.wait_recv)
        pl.when(has_right)(to_left.wait_recv)
    for to_right, to_left in copies:
        pl.when(has_right)(to_right.wait_send)
        pl.when(has_left)(to_left.wait_send)


def exchange(lines):
    position = lax.axis_index(("row", "col"))
    devices_total = lax.axis_size(("row", "col"))
    half = lines.shape[0] // 2
    arrived = pl.pallas_call(
        exchange_kernel,
        out_shape=jax.ShapeDtypeStruct(lines.shape, lines.dtype),
        in_specs=[pl.BlockSpec(memory_space=pl.ANY)],
        out_specs=pl.BlockSpec(memory_space=pl.ANY),
        scratch_shapes=[
            pltpu.SemaphoreType.DMA((2, CHUNKS)),
            pltpu.SemaphoreType.DMA((2, CHUNKS)),
        ],
        compiler_params=pltpu.CompilerParams(collective_id=1, has_side_effects=True),
    )(lines)
    top_half = lines[:half]
    new_top = jnp.where(position == 0, top_half, arrived[:half])
    new_bottom = jnp.where(position == devices_total - 1, top_half, arrived[half:])
    return jnp.concatenate([new_top, new_bottom], axis=0)


def summed(parts):
    total = parts[0]
    for part in parts[1:]:
        total = total + part
    return total


def per_device(factor_tiles):
    column_block = gather_columns(factor_tiles)
    gram_matrix = jnp.einsum("ni,nj->ij", column_block, column_block, precision=highest)
    rotation = inner_solve(gram_matrix)
    lines = jnp.einsum("ni,ij->jn", column_block, rotation, precision=highest)
    for round_index in range(1, OUTER):
        fresh = exchange(lines)
        gram_matrix = jnp.einsum("in,jn->ij", fresh, fresh, precision=highest)
        rotation = inner_solve(gram_matrix)
        if round_index + 1 < OUTER:
            lines = jnp.einsum("in,ij->jn", fresh, rotation, precision=highest)
        else:
            return jnp.einsum("in,ij->nj", fresh, rotation, precision=highest)


def solution(mesh):
    return jax.shard_map(
        per_device,
        mesh=mesh,
        in_specs=(P(None, "row", None, "col"),),
        out_specs=P(None, ("row", "col")),
        check_vma=False,
    )
```

```python
import jax
import jax.numpy as jnp
from jax import lax
from jax.sharding import PartitionSpec as P
from jax.experimental import pallas as pl
from jax.experimental.pallas import tpu as pltpu

MESH = pl.DeviceIdType.MESH

LOGB = 7
OUTER = 4
INNER = 8
CHUNKS = 2


damping_ratio = 0.01
highest = lax.Precision.HIGHEST


def passed_along(value, axis, steps):
    count = lax.axis_size(axis)
    leading, last = (max(0, -steps), min(count, count - steps))
    return lax.ppermute(value, axis, [(source, source + steps) for source in range(leading, last)])


def solve_kernel(g_ref, q_ref):
    order = g_ref.shape[0]
    gram_matrix = g_ref[...]
    rows = lax.broadcasted_iota(jnp.int32, (order, order), 0)
    cols = lax.broadcasted_iota(jnp.int32, (order, order), 1)
    identity = rows == cols
    accum = jnp.where(identity, 1.0, 0.0).astype(gram_matrix.dtype)
    lane_ids = lax.broadcasted_iota(jnp.int32, (8, order), 1)
    for inner_step in range(INNER):
        stride = 2 ** ((LOGB - 1 - inner_step) % LOGB)

        def lane_partner(value):
            lead = (lax.broadcasted_iota(jnp.int32, value.shape, 1) & stride) == 0
            ahead = pltpu.roll(value, order - stride, 1)
            behind = pltpu.roll(value, stride, 1)
            return jnp.where(lead, ahead, behind)

        def row_partner(value):
            lead = (lax.broadcasted_iota(jnp.int32, value.shape, 0) & stride) == 0
            ahead = pltpu.roll(value, order - stride, 0)
            behind = pltpu.roll(value, stride, 0)
            return jnp.where(lead, ahead, behind)

        lane_lead = (lane_ids & stride) == 0
        diagonal = jnp.broadcast_to(
            jnp.sum(jnp.where(identity, gram_matrix, 0.0), axis=0, keepdims=True), (8, order)
        )
        cross_tail = jnp.broadcast_to(
            jnp.sum(jnp.where(rows == (cols ^ stride), gram_matrix, 0.0), axis=0, keepdims=True),
            (8, order),
        )
        diag_other = lane_partner(diagonal)
        diag_p = jnp.where(lane_lead, diagonal, diag_other)
        diag_q = jnp.where(lane_lead, diag_other, diagonal)
        cross = jnp.where(lane_lead, lane_partner(cross_tail), cross_tail)
        diag_gap = diag_q - diag_p
        diag_sum = diag_p + diag_q
        rot_angle = 0.5 * jnp.arctan2(
            2.0 * cross * diag_gap, diag_gap * diag_gap + damping_ratio * diag_sum * diag_sum
        )
        cosine = jnp.cos(rot_angle)
        sine_val = jnp.sin(rot_angle)
        signed_sine = jnp.where(lane_lead, -sine_val, sine_val)
        cos_lane = jnp.broadcast_to(cosine[:1], (order, order))
        sin_lane = jnp.broadcast_to(signed_sine[:1], (order, order))
        cos_row = jnp.sum(jnp.where(identity, cos_lane, 0.0), axis=1, keepdims=True)
        sin_row = jnp.sum(jnp.where(identity, sin_lane, 0.0), axis=1, keepdims=True)
        gram_matrix = cos_lane * gram_matrix + sin_lane * lane_partner(gram_matrix)
        gram_matrix = cos_row * gram_matrix + sin_row * row_partner(gram_matrix)
        accum = cos_lane * accum + sin_lane * lane_partner(accum)
    q_ref[...] = accum


def inner_solve(gram_matrix):
    return pl.pallas_call(
        solve_kernel,
        out_shape=jax.ShapeDtypeStruct(gram_matrix.shape, gram_matrix.dtype),
    )(gram_matrix)


def relayout(tile_work):
    cycles, row_count, tile_count, tile_width = tile_work.shape
    split_view = tile_work.reshape(cycles, 1, row_count, tile_count, tile_width)
    received = lax.all_to_all(split_view, "row", split_axis=3, concat_axis=1, tiled=True)
    return received.reshape(cycles * received.shape[1] * row_count, tile_width)


def gather_kernel(src_ref, out_ref, zero_buf, send_sem, recv_sem, local_sem, zero_sem):
    cycles, height, tiles, width = src_ref.shape
    me_r = lax.axis_index("row")
    me_c = lax.axis_index("col")
    n_c = lax.axis_size("col")
    k_me = me_r * n_c + me_c

    barrier = pltpu.get_barrier_semaphore()
    for t in range(tiles):
        @pl.when(me_r != t)
        def _():
            pl.semaphore_signal(barrier, inc=1, device_id=(t, me_c), device_id_type=MESH)
    pl.semaphore_wait(barrier, tiles - 1)

    def rows_of(block):
        return out_ref.at[pl.ds(pl.multiple_of(block * height, height), height)]

    sends = []
    locals_ = []
    for i in range(cycles):
        block = i * tiles + me_r
        local = pltpu.make_async_copy(src_ref.at[i, :, me_r, :], rows_of(block), local_sem.at[i])
        pl.when(block <= k_me)(local.start)
        locals_.append((block <= k_me, local))
        for t in range(tiles):
            wanted = (block <= t * n_c + me_c) & (me_r != t)
            copy = pltpu.make_async_remote_copy(
                src_ref=src_ref.at[i, :, t, :],
                dst_ref=rows_of(block),
                send_sem=send_sem.at[t, i],
                recv_sem=recv_sem.at[me_r, i],
                device_id=(t, me_c),
                device_id_type=MESH,
            )
            pl.when(wanted)(copy.start)
            sends.append((wanted, copy))
    zero_buf[...] = jnp.zeros_like(zero_buf)
    zeros = []
    for i in range(cycles):
        for r in range(tiles):
            block = i * tiles + r
            fill = pltpu.make_async_copy(zero_buf, rows_of(block), zero_sem.at[r, i])
            pl.when(block > k_me)(fill.start)
            zeros.append((block > k_me, fill))
    for i in range(cycles):
        for r in range(tiles):
            block = i * tiles + r
            wanted = (block <= k_me) & (me_r != r)
            incoming = pltpu.make_async_remote_copy(
                src_ref=src_ref.at[i, :, r, :],
                dst_ref=rows_of(block),
                send_sem=send_sem.at[r, i],
                recv_sem=recv_sem.at[r, i],
                device_id=(r, me_c),
                device_id_type=MESH,
            )
            pl.when(wanted)(incoming.wait_recv)
    for wanted, copy in sends:
        pl.when(wanted)(copy.wait_send)
    for wanted, copy in locals_ + zeros:
        pl.when(wanted)(copy.wait)


def gather_columns(factor_tiles):
    cycles, height, tiles, width = factor_tiles.shape
    return pl.pallas_call(
        gather_kernel,
        out_shape=jax.ShapeDtypeStruct((cycles * tiles * height, width), factor_tiles.dtype),
        in_specs=[pl.BlockSpec(memory_space=pl.ANY)],
        out_specs=pl.BlockSpec(memory_space=pl.ANY),
        scratch_shapes=[
            pltpu.VMEM((height, width), factor_tiles.dtype),
            pltpu.SemaphoreType.DMA((tiles, cycles)),
            pltpu.SemaphoreType.DMA((tiles, cycles)),
            pltpu.SemaphoreType.DMA((cycles,)),
            pltpu.SemaphoreType.DMA((tiles, cycles)),
        ],
        compiler_params=pltpu.CompilerParams(collective_id=0, has_side_effects=True),
    )(factor_tiles)


def summed(parts):
    total = parts[0]
    for part in parts[1:]:
        total = total + part
    return total


def per_device(factor_tiles):
    half_width = factor_tiles.shape[-1] // 2
    column_block = gather_columns(factor_tiles)
    rows = column_block.shape[0]
    span = rows // CHUNKS
    position = lax.axis_index(("row", "col"))
    devices_total = lax.axis_size(("row", "col"))
    first = position == 0
    last = position == devices_total - 1
    pieces = [column_block[j * span:(j + 1) * span] for j in range(CHUNKS)]
    gram_matrix = jnp.einsum("ni,nj->ij", column_block, column_block, precision=highest)
    rotation = inner_solve(gram_matrix)
    lines = [jnp.einsum("ni,ij->jn", piece, rotation, precision=highest) for piece in pieces]
    for round_index in range(1, OUTER):
        fresh = []
        for piece in lines:
            top_half = piece[:half_width]
            bottom_half = piece[half_width:]
            outgoing = jnp.where(first, bottom_half, top_half)
            arrived = passed_along(outgoing, ("row", "col"), 1)
            behind = passed_along(bottom_half, ("row", "col"), -1)
            new_top = jnp.where(first, top_half, arrived)
            new_bottom = jnp.where(last, top_half, behind)
            fresh.append(jnp.concatenate([new_top, new_bottom], axis=0))
        gram_matrix = summed(
            [jnp.einsum("in,jn->ij", piece, piece, precision=highest) for piece in fresh]
        )
        rotation = inner_solve(gram_matrix)
        if round_index + 1 < OUTER:
            lines = [jnp.einsum("in,ij->jn", piece, rotation, precision=highest) for piece in fresh]
        else:
            whole = jnp.concatenate(fresh, axis=1)
            return jnp.einsum("in,ij->nj", whole, rotation, precision=highest)


def solution(mesh):
    return jax.shard_map(
        per_device,
        mesh=mesh,
        in_specs=(P(None, "row", None, "col"),),
        out_specs=P(None, ("row", "col")),
        check_vma=False,
    )
```

```python
import jax
import jax.numpy as jnp
from jax import lax
from jax.sharding import PartitionSpec as P
from jax.experimental import pallas as pl
from jax.experimental.pallas import tpu as pltpu

MESH = pl.DeviceIdType.MESH

LOGB = 7
OUTER = 4
INNER = 8
CHUNKS = 2


damping_ratio = 0.01
highest = lax.Precision.HIGHEST


def passed_along(value, axis, steps):
    count = lax.axis_size(axis)
    leading, last = (max(0, -steps), min(count, count - steps))
    return lax.ppermute(value, axis, [(source, source + steps) for source in range(leading, last)])


def solve_kernel(g_ref, q_ref):
    order = g_ref.shape[0]
    gram_matrix = g_ref[...]
    rows = lax.broadcasted_iota(jnp.int32, (order, order), 0)
    cols = lax.broadcasted_iota(jnp.int32, (order, order), 1)
    identity = rows == cols
    accum = jnp.where(identity, 1.0, 0.0).astype(gram_matrix.dtype)
    lane_ids = lax.broadcasted_iota(jnp.int32, (8, order), 1)
    for inner_step in range(INNER):
        stride = 2 ** ((LOGB - 1 - inner_step) % LOGB)

        def lane_partner(value):
            lead = (lax.broadcasted_iota(jnp.int32, value.shape, 1) & stride) == 0
            ahead = pltpu.roll(value, order - stride, 1)
            behind = pltpu.roll(value, stride, 1)
            return jnp.where(lead, ahead, behind)

        def row_partner(value):
            lead = (lax.broadcasted_iota(jnp.int32, value.shape, 0) & stride) == 0
            ahead = pltpu.roll(value, order - stride, 0)
            behind = pltpu.roll(value, stride, 0)
            return jnp.where(lead, ahead, behind)

        lane_lead = (lane_ids & stride) == 0
        diagonal = jnp.broadcast_to(
            jnp.sum(jnp.where(identity, gram_matrix, 0.0), axis=0, keepdims=True), (8, order)
        )
        cross_tail = jnp.broadcast_to(
            jnp.sum(jnp.where(rows == (cols ^ stride), gram_matrix, 0.0), axis=0, keepdims=True),
            (8, order),
        )
        diag_other = lane_partner(diagonal)
        diag_p = jnp.where(lane_lead, diagonal, diag_other)
        diag_q = jnp.where(lane_lead, diag_other, diagonal)
        cross = jnp.where(lane_lead, lane_partner(cross_tail), cross_tail)
        diag_gap = diag_q - diag_p
        diag_sum = diag_p + diag_q
        rot_angle = 0.5 * jnp.arctan2(
            2.0 * cross * diag_gap, diag_gap * diag_gap + damping_ratio * diag_sum * diag_sum
        )
        cosine = jnp.cos(rot_angle)
        sine_val = jnp.sin(rot_angle)
        signed_sine = jnp.where(lane_lead, -sine_val, sine_val)
        cos_lane = jnp.broadcast_to(cosine[:1], (order, order))
        sin_lane = jnp.broadcast_to(signed_sine[:1], (order, order))
        cos_row = jnp.sum(jnp.where(identity, cos_lane, 0.0), axis=1, keepdims=True)
        sin_row = jnp.sum(jnp.where(identity, sin_lane, 0.0), axis=1, keepdims=True)
        gram_matrix = cos_lane * gram_matrix + sin_lane * lane_partner(gram_matrix)
        gram_matrix = cos_row * gram_matrix + sin_row * row_partner(gram_matrix)
        accum = cos_lane * accum + sin_lane * lane_partner(accum)
    q_ref[...] = accum


def inner_solve(gram_matrix):
    return pl.pallas_call(
        solve_kernel,
        out_shape=jax.ShapeDtypeStruct(gram_matrix.shape, gram_matrix.dtype),
    )(gram_matrix)


def relayout(tile_work):
    cycles, row_count, tile_count, tile_width = tile_work.shape
    split_view = tile_work.reshape(cycles, 1, row_count, tile_count, tile_width)
    received = lax.all_to_all(split_view, "row", split_axis=3, concat_axis=1, tiled=True)
    return received.reshape(cycles * received.shape[1] * row_count, tile_width)


def gather_kernel(src_ref, out_ref, land, send_sem, recv_sem, local_sem):
    cycles, height, tiles, width = src_ref.shape
    me_r = lax.axis_index("row")
    me_c = lax.axis_index("col")
    n_c = lax.axis_size("col")
    k_me = me_r * n_c + me_c

    barrier = pltpu.get_barrier_semaphore()
    for t in range(tiles):
        @pl.when(me_r != t)
        def _():
            pl.semaphore_signal(barrier, inc=1, device_id=(t, me_c), device_id_type=MESH)
    pl.semaphore_wait(barrier, tiles - 1)

    def rows_of(block):
        return land.at[pl.ds(pl.multiple_of(block * height, height), height)]

    sends = []
    for i in range(cycles):
        block = i * tiles + me_r
        local = pltpu.make_async_copy(src_ref.at[i, :, me_r, :], rows_of(block), local_sem.at[i])
        pl.when(block <= k_me)(local.start)
        for t in range(tiles):
            wanted = (block <= t * n_c + me_c) & (me_r != t)
            copy = pltpu.make_async_remote_copy(
                src_ref=src_ref.at[i, :, t, :],
                dst_ref=rows_of(block),
                send_sem=send_sem.at[t, i],
                recv_sem=recv_sem.at[me_r, i],
                device_id=(t, me_c),
                device_id_type=MESH,
            )
            pl.when(wanted)(copy.start)
            sends.append((wanted, copy))
    for i in range(cycles):
        for r in range(tiles):
            block = i * tiles + r
            columns = slice(block * height, (block + 1) * height)
            incoming = pltpu.make_async_remote_copy(
                src_ref=src_ref.at[i, :, r, :],
                dst_ref=land.at[columns],
                send_sem=send_sem.at[r, i],
                recv_sem=recv_sem.at[r, i],
                device_id=(r, me_c),
                device_id_type=MESH,
            )
            local = pltpu.make_async_copy(src_ref.at[i, :, r, :], land.at[columns], local_sem.at[i])
            pl.when((block <= k_me) & (me_r != r))(incoming.wait_recv)
            pl.when((block <= k_me) & (me_r == r))(local.wait)

            @pl.when(block <= k_me)
            def _():
                out_ref[:, columns] = land[columns, :].T

            @pl.when(block > k_me)
            def _():
                out_ref[:, columns] = jnp.zeros((width, height), out_ref.dtype)

    for wanted, copy in sends:
        pl.when(wanted)(copy.wait_send)


def gather_columns(factor_tiles):
    cycles, height, tiles, width = factor_tiles.shape
    return pl.pallas_call(
        gather_kernel,
        out_shape=jax.ShapeDtypeStruct((width, cycles * tiles * height), factor_tiles.dtype),
        in_specs=[pl.BlockSpec(memory_space=pl.ANY)],
        out_specs=pl.BlockSpec(memory_space=pltpu.VMEM),
        scratch_shapes=[
            pltpu.VMEM((cycles * tiles * height, width), factor_tiles.dtype),
            pltpu.SemaphoreType.DMA((tiles, cycles)),
            pltpu.SemaphoreType.DMA((tiles, cycles)),
            pltpu.SemaphoreType.DMA((cycles,)),
        ],
        compiler_params=pltpu.CompilerParams(
            collective_id=0, has_side_effects=True, vmem_limit_bytes=48 * 1024 * 1024
        ),
    )(factor_tiles)


def summed(parts):
    total = parts[0]
    for part in parts[1:]:
        total = total + part
    return total


def per_device(factor_tiles):
    half_width = factor_tiles.shape[-1] // 2
    column_lines = gather_columns(factor_tiles)
    rows = column_lines.shape[1]
    span = rows // CHUNKS
    position = lax.axis_index(("row", "col"))
    devices_total = lax.axis_size(("row", "col"))
    first = position == 0
    last = position == devices_total - 1
    pieces = [column_lines[:, j * span:(j + 1) * span] for j in range(CHUNKS)]
    gram_matrix = jnp.einsum("in,jn->ij", column_lines, column_lines, precision=highest)
    rotation = inner_solve(gram_matrix)
    lines = [jnp.einsum("in,ij->jn", piece, rotation, precision=highest) for piece in pieces]
    for round_index in range(1, OUTER):
        fresh = []
        for piece in lines:
            top_half = piece[:half_width]
            bottom_half = piece[half_width:]
            outgoing = jnp.where(first, bottom_half, top_half)
            arrived = passed_along(outgoing, ("row", "col"), 1)
            behind = passed_along(bottom_half, ("row", "col"), -1)
            new_top = jnp.where(first, top_half, arrived)
            new_bottom = jnp.where(last, top_half, behind)
            fresh.append(jnp.concatenate([new_top, new_bottom], axis=0))
        gram_matrix = summed(
            [jnp.einsum("in,jn->ij", piece, piece, precision=highest) for piece in fresh]
        )
        rotation = inner_solve(gram_matrix)
        if round_index + 1 < OUTER:
            lines = [jnp.einsum("in,ij->jn", piece, rotation, precision=highest) for piece in fresh]
        else:
            whole = jnp.concatenate(fresh, axis=1)
            return jnp.einsum("in,ij->nj", whole, rotation, precision=highest)


def solution(mesh):
    return jax.shard_map(
        per_device,
        mesh=mesh,
        in_specs=(P(None, "row", None, "col"),),
        out_specs=P(None, ("row", "col")),
        check_vma=False,
    )
```

```python
import jax
import jax.numpy as jnp
from jax import lax
from jax.sharding import PartitionSpec as P
from jax.experimental import pallas as pl
from jax.experimental.pallas import tpu as pltpu

MESH = pl.DeviceIdType.MESH

LOGB = 7
OUTER = 4
INNER = 8
CHUNKS = 2


damping_ratio = 0.01
highest = lax.Precision.HIGHEST


def passed_along(value, axis, steps):
    count = lax.axis_size(axis)
    leading, last = (max(0, -steps), min(count, count - steps))
    return lax.ppermute(value, axis, [(source, source + steps) for source in range(leading, last)])


def solve_kernel(g_ref, q_ref):
    order = g_ref.shape[0]
    gram_matrix = g_ref[...]
    rows = lax.broadcasted_iota(jnp.int32, (order, order), 0)
    cols = lax.broadcasted_iota(jnp.int32, (order, order), 1)
    identity = rows == cols
    accum = jnp.where(identity, 1.0, 0.0).astype(gram_matrix.dtype)
    lane_ids = lax.broadcasted_iota(jnp.int32, (8, order), 1)
    for inner_step in range(INNER):
        stride = 2 ** ((LOGB - 1 - inner_step) % LOGB)

        def lane_partner(value):
            lead = (lax.broadcasted_iota(jnp.int32, value.shape, 1) & stride) == 0
            ahead = pltpu.roll(value, order - stride, 1)
            behind = pltpu.roll(value, stride, 1)
            return jnp.where(lead, ahead, behind)

        def row_partner(value):
            lead = (lax.broadcasted_iota(jnp.int32, value.shape, 0) & stride) == 0
            ahead = pltpu.roll(value, order - stride, 0)
            behind = pltpu.roll(value, stride, 0)
            return jnp.where(lead, ahead, behind)

        lane_lead = (lane_ids & stride) == 0
        diagonal = jnp.broadcast_to(
            jnp.sum(jnp.where(identity, gram_matrix, 0.0), axis=0, keepdims=True), (8, order)
        )
        cross_tail = jnp.broadcast_to(
            jnp.sum(jnp.where(rows == (cols ^ stride), gram_matrix, 0.0), axis=0, keepdims=True),
            (8, order),
        )
        diag_other = lane_partner(diagonal)
        diag_p = jnp.where(lane_lead, diagonal, diag_other)
        diag_q = jnp.where(lane_lead, diag_other, diagonal)
        cross = jnp.where(lane_lead, lane_partner(cross_tail), cross_tail)
        diag_gap = diag_q - diag_p
        diag_sum = diag_p + diag_q
        rot_angle = 0.5 * jnp.arctan2(
            2.0 * cross * diag_gap, diag_gap * diag_gap + damping_ratio * diag_sum * diag_sum
        )
        cosine = jnp.cos(rot_angle)
        sine_val = jnp.sin(rot_angle)
        signed_sine = jnp.where(lane_lead, -sine_val, sine_val)
        cos_lane = jnp.broadcast_to(cosine[:1], (order, order))
        sin_lane = jnp.broadcast_to(signed_sine[:1], (order, order))
        cos_row = jnp.sum(jnp.where(identity, cos_lane, 0.0), axis=1, keepdims=True)
        sin_row = jnp.sum(jnp.where(identity, sin_lane, 0.0), axis=1, keepdims=True)
        gram_matrix = cos_lane * gram_matrix + sin_lane * lane_partner(gram_matrix)
        gram_matrix = cos_row * gram_matrix + sin_row * row_partner(gram_matrix)
        accum = cos_lane * accum + sin_lane * lane_partner(accum)
    q_ref[...] = accum


def inner_solve(gram_matrix):
    return pl.pallas_call(
        solve_kernel,
        out_shape=jax.ShapeDtypeStruct(gram_matrix.shape, gram_matrix.dtype),
    )(gram_matrix)


def relayout(tile_work):
    cycles, row_count, tile_count, tile_width = tile_work.shape
    split_view = tile_work.reshape(cycles, 1, row_count, tile_count, tile_width)
    received = lax.all_to_all(split_view, "row", split_axis=3, concat_axis=1, tiled=True)
    return received.reshape(cycles * received.shape[1] * row_count, tile_width)


def gather_kernel(src_ref, out_ref, land, send_sem, recv_sem, local_sem):
    cycles, height, tiles, width = src_ref.shape
    me_r = lax.axis_index("row")
    me_c = lax.axis_index("col")
    n_c = lax.axis_size("col")
    k_me = me_r * n_c + me_c

    barrier = pltpu.get_barrier_semaphore()
    for t in range(tiles):
        @pl.when(me_r != t)
        def _():
            pl.semaphore_signal(barrier, inc=1, device_id=(t, me_c), device_id_type=MESH)
    pl.semaphore_wait(barrier, tiles - 1)

    def rows_of(block):
        return land.at[pl.ds(pl.multiple_of(block * height, height), height)]

    sends = []
    for i in range(cycles):
        block = i * tiles + me_r
        local = pltpu.make_async_copy(src_ref.at[i, :, me_r, :], rows_of(block), local_sem.at[i])
        pl.when(block <= k_me)(local.start)
        for t in range(tiles):
            wanted = (block <= t * n_c + me_c) & (me_r != t)
            copy = pltpu.make_async_remote_copy(
                src_ref=src_ref.at[i, :, t, :],
                dst_ref=rows_of(block),
                send_sem=send_sem.at[t, i],
                recv_sem=recv_sem.at[me_r, i],
                device_id=(t, me_c),
                device_id_type=MESH,
            )
            pl.when(wanted)(copy.start)
            sends.append((wanted, copy))
    for i in range(cycles):
        for r in range(tiles):
            block = i * tiles + r
            columns = slice(block * height, (block + 1) * height)
            incoming = pltpu.make_async_remote_copy(
                src_ref=src_ref.at[i, :, r, :],
                dst_ref=land.at[columns],
                send_sem=send_sem.at[r, i],
                recv_sem=recv_sem.at[r, i],
                device_id=(r, me_c),
                device_id_type=MESH,
            )
            local = pltpu.make_async_copy(src_ref.at[i, :, r, :], land.at[columns], local_sem.at[i])
            pl.when((block <= k_me) & (me_r != r))(incoming.wait_recv)
            pl.when((block <= k_me) & (me_r == r))(local.wait)

            @pl.when(block <= k_me)
            def _():
                out_ref[:, columns] = land[columns, :].T

            @pl.when(block > k_me)
            def _():
                out_ref[:, columns] = jnp.zeros((width, height), out_ref.dtype)

    for wanted, copy in sends:
        pl.when(wanted)(copy.wait_send)


def gather_columns(factor_tiles):
    cycles, height, tiles, width = factor_tiles.shape
    return pl.pallas_call(
        gather_kernel,
        out_shape=jax.ShapeDtypeStruct((width, cycles * tiles * height), factor_tiles.dtype),
        in_specs=[pl.BlockSpec(memory_space=pl.ANY)],
        out_specs=pl.BlockSpec(memory_space=pltpu.VMEM),
        scratch_shapes=[
            pltpu.VMEM((cycles * tiles * height, width), factor_tiles.dtype),
            pltpu.SemaphoreType.DMA((tiles, cycles)),
            pltpu.SemaphoreType.DMA((tiles, cycles)),
            pltpu.SemaphoreType.DMA((cycles,)),
        ],
        compiler_params=pltpu.CompilerParams(
            collective_id=0, has_side_effects=True, vmem_limit_bytes=48 * 1024 * 1024
        ),
    )(factor_tiles)


def summed(parts):
    total = parts[0]
    for part in parts[1:]:
        total = total + part
    return total


def per_device(factor_tiles):
    half_width = factor_tiles.shape[-1] // 2
    column_lines = gather_columns(factor_tiles)
    rows = column_lines.shape[1]
    span = rows // CHUNKS
    position = lax.axis_index(("row", "col"))
    devices_total = lax.axis_size(("row", "col"))
    first = position == 0
    last = position == devices_total - 1
    pieces = [column_lines[:, j * span:(j + 1) * span] for j in range(CHUNKS)]
    gram_matrix = jnp.einsum("in,jn->ij", column_lines, column_lines, precision=highest)
    rotation = inner_solve(gram_matrix)
    def sending(rotation):
        return jnp.where(first, jnp.roll(rotation, half_width, axis=1), rotation)

    lines = [jnp.einsum("in,ij->jn", piece, sending(rotation), precision=highest) for piece in pieces]
    for round_index in range(1, OUTER):
        fresh = []
        for piece in lines:
            outgoing = piece[:half_width]
            kept = piece[half_width:]
            arrived = passed_along(outgoing, ("row", "col"), 1)
            behind = passed_along(kept, ("row", "col"), -1)
            new_top = jnp.where(first, kept, arrived)
            new_bottom = jnp.where(last, outgoing, behind)
            fresh.append(jnp.concatenate([new_top, new_bottom], axis=0))
        gram_matrix = summed(
            [jnp.einsum("in,jn->ij", piece, piece, precision=highest) for piece in fresh]
        )
        rotation = inner_solve(gram_matrix)
        if round_index + 1 < OUTER:
            lines = [
                jnp.einsum("in,ij->jn", piece, sending(rotation), precision=highest) for piece in fresh
            ]
        else:
            whole = jnp.concatenate(fresh, axis=1)
            return jnp.einsum("in,ij->nj", whole, rotation, precision=highest)


def solution(mesh):
    return jax.shard_map(
        per_device,
        mesh=mesh,
        in_specs=(P(None, "row", None, "col"),),
        out_specs=P(None, ("row", "col")),
        check_vma=False,
    )
```

```python
import jax
import jax.numpy as jnp
from jax import lax
from jax.sharding import PartitionSpec as P
from jax.experimental import pallas as pl
from jax.experimental.pallas import tpu as pltpu

MESH = pl.DeviceIdType.MESH

LOGB = 7
OUTER = 4
INNER = 8
CHUNKS = 2


damping_ratio = 0.01
highest = lax.Precision.HIGHEST


def passed_along(value, axis, steps):
    count = lax.axis_size(axis)
    leading, last = (max(0, -steps), min(count, count - steps))
    return lax.ppermute(value, axis, [(source, source + steps) for source in range(leading, last)])


def solve_kernel(g_ref, q_ref):
    order = g_ref.shape[0]
    gram_matrix = g_ref[...]
    rows = lax.broadcasted_iota(jnp.int32, (order, order), 0)
    cols = lax.broadcasted_iota(jnp.int32, (order, order), 1)
    identity = rows == cols
    accum = jnp.where(identity, 1.0, 0.0).astype(gram_matrix.dtype)
    lane_ids = lax.broadcasted_iota(jnp.int32, (8, order), 1)
    for inner_step in range(INNER):
        stride = 2 ** ((LOGB - 1 - inner_step) % LOGB)

        def lane_partner(value):
            lead = (lax.broadcasted_iota(jnp.int32, value.shape, 1) & stride) == 0
            ahead = pltpu.roll(value, order - stride, 1)
            behind = pltpu.roll(value, stride, 1)
            return jnp.where(lead, ahead, behind)

        def row_partner(value):
            lead = (lax.broadcasted_iota(jnp.int32, value.shape, 0) & stride) == 0
            ahead = pltpu.roll(value, order - stride, 0)
            behind = pltpu.roll(value, stride, 0)
            return jnp.where(lead, ahead, behind)

        lane_lead = (lane_ids & stride) == 0
        diagonal = jnp.broadcast_to(
            jnp.sum(jnp.where(identity, gram_matrix, 0.0), axis=0, keepdims=True), (8, order)
        )
        cross_tail = jnp.broadcast_to(
            jnp.sum(jnp.where(rows == (cols ^ stride), gram_matrix, 0.0), axis=0, keepdims=True),
            (8, order),
        )
        diag_other = lane_partner(diagonal)
        diag_p = jnp.where(lane_lead, diagonal, diag_other)
        diag_q = jnp.where(lane_lead, diag_other, diagonal)
        cross = jnp.where(lane_lead, lane_partner(cross_tail), cross_tail)
        diag_gap = diag_q - diag_p
        diag_sum = diag_p + diag_q
        rot_angle = 0.5 * jnp.arctan2(
            2.0 * cross * diag_gap, diag_gap * diag_gap + damping_ratio * diag_sum * diag_sum
        )
        cosine = jnp.cos(rot_angle)
        sine_val = jnp.sin(rot_angle)
        signed_sine = jnp.where(lane_lead, -sine_val, sine_val)
        cos_lane = jnp.broadcast_to(cosine[:1], (order, order))
        sin_lane = jnp.broadcast_to(signed_sine[:1], (order, order))
        cos_row = jnp.sum(jnp.where(identity, cos_lane, 0.0), axis=1, keepdims=True)
        sin_row = jnp.sum(jnp.where(identity, sin_lane, 0.0), axis=1, keepdims=True)
        gram_matrix = cos_lane * gram_matrix + sin_lane * lane_partner(gram_matrix)
        gram_matrix = cos_row * gram_matrix + sin_row * row_partner(gram_matrix)
        accum = cos_lane * accum + sin_lane * lane_partner(accum)
    q_ref[...] = accum


def inner_solve(gram_matrix):
    return pl.pallas_call(
        solve_kernel,
        out_shape=jax.ShapeDtypeStruct(gram_matrix.shape, gram_matrix.dtype),
    )(gram_matrix)


def relayout(tile_work):
    cycles, row_count, tile_count, tile_width = tile_work.shape
    split_view = tile_work.reshape(cycles, 1, row_count, tile_count, tile_width)
    received = lax.all_to_all(split_view, "row", split_axis=3, concat_axis=1, tiled=True)
    return received.reshape(cycles * received.shape[1] * row_count, tile_width)


def gather_kernel(src_ref, out_ref, gram_ref, land, send_sem, recv_sem, local_sem):
    cycles, height, tiles, width = src_ref.shape
    me_r = lax.axis_index("row")
    me_c = lax.axis_index("col")
    n_c = lax.axis_size("col")
    k_me = me_r * n_c + me_c

    barrier = pltpu.get_barrier_semaphore()
    for t in range(tiles):
        @pl.when(me_r != t)
        def _():
            pl.semaphore_signal(barrier, inc=1, device_id=(t, me_c), device_id_type=MESH)
    pl.semaphore_wait(barrier, tiles - 1)

    def rows_of(block):
        return land.at[pl.ds(pl.multiple_of(block * height, height), height)]

    sends = []
    for i in range(cycles):
        block = i * tiles + me_r
        local = pltpu.make_async_copy(src_ref.at[i, :, me_r, :], rows_of(block), local_sem.at[i])
        pl.when(block <= k_me)(local.start)
        for t in range(tiles):
            wanted = (block <= t * n_c + me_c) & (me_r != t)
            copy = pltpu.make_async_remote_copy(
                src_ref=src_ref.at[i, :, t, :],
                dst_ref=rows_of(block),
                send_sem=send_sem.at[t, i],
                recv_sem=recv_sem.at[me_r, i],
                device_id=(t, me_c),
                device_id_type=MESH,
            )
            pl.when(wanted)(copy.start)
            sends.append((wanted, copy))
    gram_ref[...] = jnp.zeros_like(gram_ref)
    for i in range(cycles):
        for r in range(tiles):
            block = i * tiles + r
            columns = slice(block * height, (block + 1) * height)
            incoming = pltpu.make_async_remote_copy(
                src_ref=src_ref.at[i, :, r, :],
                dst_ref=land.at[columns],
                send_sem=send_sem.at[r, i],
                recv_sem=recv_sem.at[r, i],
                device_id=(r, me_c),
                device_id_type=MESH,
            )
            local = pltpu.make_async_copy(src_ref.at[i, :, r, :], land.at[columns], local_sem.at[i])
            pl.when((block <= k_me) & (me_r != r))(incoming.wait_recv)
            pl.when((block <= k_me) & (me_r == r))(local.wait)

            @pl.when(block <= k_me)
            def _():
                rows_in = land[columns, :]
                lines_in = rows_in.T
                out_ref[:, columns] = lines_in
                gram_ref[...] += jnp.dot(
                    lines_in, rows_in, precision=highest, preferred_element_type=jnp.float32
                )

            @pl.when(block > k_me)
            def _():
                out_ref[:, columns] = jnp.zeros((width, height), out_ref.dtype)

    for wanted, copy in sends:
        pl.when(wanted)(copy.wait_send)


def gather_columns(factor_tiles):
    cycles, height, tiles, width = factor_tiles.shape
    return pl.pallas_call(
        gather_kernel,
        out_shape=(
            jax.ShapeDtypeStruct((width, cycles * tiles * height), factor_tiles.dtype),
            jax.ShapeDtypeStruct((width, width), factor_tiles.dtype),
        ),
        in_specs=[pl.BlockSpec(memory_space=pl.ANY)],
        out_specs=(
            pl.BlockSpec(memory_space=pltpu.VMEM),
            pl.BlockSpec(memory_space=pltpu.VMEM),
        ),
        scratch_shapes=[
            pltpu.VMEM((cycles * tiles * height, width), factor_tiles.dtype),
            pltpu.SemaphoreType.DMA((tiles, cycles)),
            pltpu.SemaphoreType.DMA((tiles, cycles)),
            pltpu.SemaphoreType.DMA((cycles,)),
        ],
        compiler_params=pltpu.CompilerParams(
            collective_id=0, has_side_effects=True, vmem_limit_bytes=48 * 1024 * 1024
        ),
    )(factor_tiles)


def summed(parts):
    total = parts[0]
    for part in parts[1:]:
        total = total + part
    return total


def per_device(factor_tiles):
    half_width = factor_tiles.shape[-1] // 2
    column_lines, gram_matrix = gather_columns(factor_tiles)
    rows = column_lines.shape[1]
    span = rows // CHUNKS
    position = lax.axis_index(("row", "col"))
    devices_total = lax.axis_size(("row", "col"))
    first = position == 0
    last = position == devices_total - 1
    pieces = [column_lines[:, j * span:(j + 1) * span] for j in range(CHUNKS)]
    rotation = inner_solve(gram_matrix)
    lines = [jnp.einsum("in,ij->jn", piece, rotation, precision=highest) for piece in pieces]
    for round_index in range(1, OUTER):
        fresh = []
        for piece in lines:
            top_half = piece[:half_width]
            bottom_half = piece[half_width:]
            outgoing = jnp.where(first, bottom_half, top_half)
            arrived = passed_along(outgoing, ("row", "col"), 1)
            behind = passed_along(bottom_half, ("row", "col"), -1)
            new_top = jnp.where(first, top_half, arrived)
            new_bottom = jnp.where(last, top_half, behind)
            fresh.append(jnp.concatenate([new_top, new_bottom], axis=0))
        gram_matrix = summed(
            [jnp.einsum("in,jn->ij", piece, piece, precision=highest) for piece in fresh]
        )
        rotation = inner_solve(gram_matrix)
        if round_index + 1 < OUTER:
            lines = [jnp.einsum("in,ij->jn", piece, rotation, precision=highest) for piece in fresh]
        else:
            whole = jnp.concatenate(fresh, axis=1)
            return jnp.einsum("in,ij->nj", whole, rotation, precision=highest)


def solution(mesh):
    return jax.shard_map(
        per_device,
        mesh=mesh,
        in_specs=(P(None, "row", None, "col"),),
        out_specs=P(None, ("row", "col")),
        check_vma=False,
    )
```

```python
import jax
import jax.numpy as jnp
from jax import lax
from jax.sharding import PartitionSpec as P
from jax.experimental import pallas as pl
from jax.experimental.pallas import tpu as pltpu

MESH = pl.DeviceIdType.MESH

LOGB = 7
OUTER = 4
INNER = 8
CHUNKS = 2


damping_ratio = 0.01
highest = lax.Precision.HIGHEST


def passed_along(value, axis, steps):
    count = lax.axis_size(axis)
    leading, last = (max(0, -steps), min(count, count - steps))
    return lax.ppermute(value, axis, [(source, source + steps) for source in range(leading, last)])


def solve_kernel(g_ref, q_ref):
    order = g_ref.shape[0]
    gram_matrix = g_ref[...]
    rows = lax.broadcasted_iota(jnp.int32, (order, order), 0)
    cols = lax.broadcasted_iota(jnp.int32, (order, order), 1)
    identity = rows == cols
    accum = jnp.where(identity, 1.0, 0.0).astype(gram_matrix.dtype)
    lane_ids = lax.broadcasted_iota(jnp.int32, (8, order), 1)
    for inner_step in range(INNER):
        stride = 2 ** ((LOGB - 1 - inner_step) % LOGB)

        def lane_partner(value):
            lead = (lax.broadcasted_iota(jnp.int32, value.shape, 1) & stride) == 0
            ahead = pltpu.roll(value, order - stride, 1)
            behind = pltpu.roll(value, stride, 1)
            return jnp.where(lead, ahead, behind)

        def row_partner(value):
            lead = (lax.broadcasted_iota(jnp.int32, value.shape, 0) & stride) == 0
            ahead = pltpu.roll(value, order - stride, 0)
            behind = pltpu.roll(value, stride, 0)
            return jnp.where(lead, ahead, behind)

        lane_lead = (lane_ids & stride) == 0
        diagonal = jnp.broadcast_to(
            jnp.sum(jnp.where(identity, gram_matrix, 0.0), axis=0, keepdims=True), (8, order)
        )
        cross_tail = jnp.broadcast_to(
            jnp.sum(jnp.where(rows == (cols ^ stride), gram_matrix, 0.0), axis=0, keepdims=True),
            (8, order),
        )
        diag_other = lane_partner(diagonal)
        diag_p = jnp.where(lane_lead, diagonal, diag_other)
        diag_q = jnp.where(lane_lead, diag_other, diagonal)
        cross = jnp.where(lane_lead, lane_partner(cross_tail), cross_tail)
        diag_gap = diag_q - diag_p
        diag_sum = diag_p + diag_q
        rot_angle = 0.5 * jnp.arctan2(
            2.0 * cross * diag_gap, diag_gap * diag_gap + damping_ratio * diag_sum * diag_sum
        )
        cosine = jnp.cos(rot_angle)
        sine_val = jnp.sin(rot_angle)
        signed_sine = jnp.where(lane_lead, -sine_val, sine_val)
        cos_lane = jnp.broadcast_to(cosine[:1], (order, order))
        sin_lane = jnp.broadcast_to(signed_sine[:1], (order, order))
        cos_row = jnp.sum(jnp.where(identity, cos_lane, 0.0), axis=1, keepdims=True)
        sin_row = jnp.sum(jnp.where(identity, sin_lane, 0.0), axis=1, keepdims=True)
        gram_matrix = cos_lane * gram_matrix + sin_lane * lane_partner(gram_matrix)
        gram_matrix = cos_row * gram_matrix + sin_row * row_partner(gram_matrix)
        accum = cos_lane * accum + sin_lane * lane_partner(accum)
    q_ref[...] = accum


def inner_solve(gram_matrix):
    return pl.pallas_call(
        solve_kernel,
        out_shape=jax.ShapeDtypeStruct(gram_matrix.shape, gram_matrix.dtype),
    )(gram_matrix)


def relayout(tile_work):
    cycles, row_count, tile_count, tile_width = tile_work.shape
    split_view = tile_work.reshape(cycles, 1, row_count, tile_count, tile_width)
    received = lax.all_to_all(split_view, "row", split_axis=3, concat_axis=1, tiled=True)
    return received.reshape(cycles * received.shape[1] * row_count, tile_width)


def gather_kernel(src_ref, out_ref, gram_ref, land, send_sem, recv_sem, local_sem):
    cycles, height, tiles, width = src_ref.shape
    me_r = lax.axis_index("row")
    me_c = lax.axis_index("col")
    n_c = lax.axis_size("col")
    k_me = me_r * n_c + me_c

    barrier = pltpu.get_barrier_semaphore()
    for t in range(tiles):
        @pl.when(me_r != t)
        def _():
            pl.semaphore_signal(barrier, inc=1, device_id=(t, me_c), device_id_type=MESH)
    pl.semaphore_wait(barrier, tiles - 1)

    def rows_of(block):
        return land.at[pl.ds(pl.multiple_of(block * height, height), height)]

    sends = []
    for i in range(cycles):
        block = i * tiles + me_r
        local = pltpu.make_async_copy(src_ref.at[i, :, me_r, :], rows_of(block), local_sem.at[i])
        pl.when(block <= k_me)(local.start)
        for t in range(tiles):
            wanted = (block <= t * n_c + me_c) & (me_r != t)
            copy = pltpu.make_async_remote_copy(
                src_ref=src_ref.at[i, :, t, :],
                dst_ref=rows_of(block),
                send_sem=send_sem.at[t, i],
                recv_sem=recv_sem.at[me_r, i],
                device_id=(t, me_c),
                device_id_type=MESH,
            )
            pl.when(wanted)(copy.start)
            sends.append((wanted, copy))
    gram_ref[...] = jnp.zeros_like(gram_ref)
    for i in range(cycles):
        for r in range(tiles):
            block = i * tiles + r
            columns = slice(block * height, (block + 1) * height)
            incoming = pltpu.make_async_remote_copy(
                src_ref=src_ref.at[i, :, r, :],
                dst_ref=land.at[columns],
                send_sem=send_sem.at[r, i],
                recv_sem=recv_sem.at[r, i],
                device_id=(r, me_c),
                device_id_type=MESH,
            )
            local = pltpu.make_async_copy(src_ref.at[i, :, r, :], land.at[columns], local_sem.at[i])
            pl.when((block <= k_me) & (me_r != r))(incoming.wait_recv)
            pl.when((block <= k_me) & (me_r == r))(local.wait)

            @pl.when(block <= k_me)
            def _():
                rows_in = land[columns, :]
                lines_in = rows_in.T
                out_ref[:, columns] = lines_in
                gram_ref[...] += jnp.dot(
                    lines_in, rows_in, precision=highest, preferred_element_type=jnp.float32
                )

            @pl.when(block > k_me)
            def _():
                out_ref[:, columns] = jnp.zeros((width, height), out_ref.dtype)

    for wanted, copy in sends:
        pl.when(wanted)(copy.wait_send)


def gather_columns(factor_tiles):
    cycles, height, tiles, width = factor_tiles.shape
    return pl.pallas_call(
        gather_kernel,
        out_shape=(
            jax.ShapeDtypeStruct((width, cycles * tiles * height), factor_tiles.dtype),
            jax.ShapeDtypeStruct((width, width), factor_tiles.dtype),
        ),
        in_specs=[pl.BlockSpec(memory_space=pl.ANY)],
        out_specs=(
            pl.BlockSpec(memory_space=pltpu.VMEM),
            pl.BlockSpec(memory_space=pltpu.VMEM),
        ),
        scratch_shapes=[
            pltpu.VMEM((cycles * tiles * height, width), factor_tiles.dtype),
            pltpu.SemaphoreType.DMA((tiles, cycles)),
            pltpu.SemaphoreType.DMA((tiles, cycles)),
            pltpu.SemaphoreType.DMA((cycles,)),
        ],
        compiler_params=pltpu.CompilerParams(
            collective_id=0, has_side_effects=True, vmem_limit_bytes=48 * 1024 * 1024
        ),
    )(factor_tiles)


def final_kernel(first_ref, second_ref, rotation_ref, out_ref):
    step = pl.program_id(0)
    half = pl.num_programs(0) // 2

    @pl.when(step < half)
    def _():
        out_ref[...] = jnp.dot(
            first_ref[...].T, rotation_ref[...], precision=highest, preferred_element_type=jnp.float32
        )

    @pl.when(step >= half)
    def _():
        out_ref[...] = jnp.dot(
            second_ref[...].T, rotation_ref[...], precision=highest, preferred_element_type=jnp.float32
        )


def final_apply(fresh, rotation):
    first, second = fresh
    order, width = first.shape
    depth = 512
    per_piece = width // depth
    return pl.pallas_call(
        final_kernel,
        grid=(2 * per_piece,),
        out_shape=jax.ShapeDtypeStruct((2 * width, order), first.dtype),
        in_specs=[
            pl.BlockSpec((order, depth), lambda g: (0, jnp.minimum(g, per_piece - 1))),
            pl.BlockSpec((order, depth), lambda g: (0, jnp.maximum(g - per_piece, 0))),
            pl.BlockSpec((order, order), lambda g: (0, 0)),
        ],
        out_specs=pl.BlockSpec((depth, order), lambda g: (g, 0)),
    )(first, second, rotation)


def summed(parts):
    total = parts[0]
    for part in parts[1:]:
        total = total + part
    return total


def per_device(factor_tiles):
    half_width = factor_tiles.shape[-1] // 2
    column_lines, gram_matrix = gather_columns(factor_tiles)
    rows = column_lines.shape[1]
    span = rows // CHUNKS
    position = lax.axis_index(("row", "col"))
    devices_total = lax.axis_size(("row", "col"))
    first = position == 0
    last = position == devices_total - 1
    pieces = [column_lines[:, j * span:(j + 1) * span] for j in range(CHUNKS)]
    rotation = inner_solve(gram_matrix)
    lines = [jnp.einsum("in,ij->jn", piece, rotation, precision=highest) for piece in pieces]
    for round_index in range(1, OUTER):
        fresh = []
        for piece in lines:
            top_half = piece[:half_width]
            bottom_half = piece[half_width:]
            outgoing = jnp.where(first, bottom_half, top_half)
            arrived = passed_along(outgoing, ("row", "col"), 1)
            behind = passed_along(bottom_half, ("row", "col"), -1)
            new_top = jnp.where(first, top_half, arrived)
            new_bottom = jnp.where(last, top_half, behind)
            fresh.append(jnp.concatenate([new_top, new_bottom], axis=0))
        gram_matrix = summed(
            [jnp.einsum("in,jn->ij", piece, piece, precision=highest) for piece in fresh]
        )
        rotation = inner_solve(gram_matrix)
        if round_index + 1 < OUTER:
            lines = [jnp.einsum("in,ij->jn", piece, rotation, precision=highest) for piece in fresh]
        else:
            return final_apply(fresh, rotation)


def solution(mesh):
    return jax.shard_map(
        per_device,
        mesh=mesh,
        in_specs=(P(None, "row", None, "col"),),
        out_specs=P(None, ("row", "col")),
        check_vma=False,
    )
```

```python
import jax
import jax.numpy as jnp
from jax import lax
from jax.sharding import PartitionSpec as P
from jax.experimental import pallas as pl
from jax.experimental.pallas import tpu as pltpu

MESH = pl.DeviceIdType.MESH

LOGB = 7
OUTER = 4
INNER = 8
CHUNKS = 2


damping_ratio = 0.01
highest = lax.Precision.HIGHEST


def passed_along(value, axis, steps):
    count = lax.axis_size(axis)
    leading, last = (max(0, -steps), min(count, count - steps))
    return lax.ppermute(value, axis, [(source, source + steps) for source in range(leading, last)])


def solve_kernel(g_ref, q_ref):
    order = g_ref.shape[0]
    gram_matrix = g_ref[...]
    rows = lax.broadcasted_iota(jnp.int32, (order, order), 0)
    cols = lax.broadcasted_iota(jnp.int32, (order, order), 1)
    identity = rows == cols
    accum = jnp.where(identity, 1.0, 0.0).astype(gram_matrix.dtype)
    lane_ids = lax.broadcasted_iota(jnp.int32, (8, order), 1)
    for inner_step in range(INNER):
        stride = 2 ** ((LOGB - 1 - inner_step) % LOGB)

        def lane_partner(value):
            lead = (lax.broadcasted_iota(jnp.int32, value.shape, 1) & stride) == 0
            ahead = pltpu.roll(value, order - stride, 1)
            behind = pltpu.roll(value, stride, 1)
            return jnp.where(lead, ahead, behind)

        def row_partner(value):
            lead = (lax.broadcasted_iota(jnp.int32, value.shape, 0) & stride) == 0
            ahead = pltpu.roll(value, order - stride, 0)
            behind = pltpu.roll(value, stride, 0)
            return jnp.where(lead, ahead, behind)

        lane_lead = (lane_ids & stride) == 0
        diagonal = jnp.broadcast_to(
            jnp.sum(jnp.where(identity, gram_matrix, 0.0), axis=0, keepdims=True), (8, order)
        )
        cross_tail = jnp.broadcast_to(
            jnp.sum(jnp.where(rows == (cols ^ stride), gram_matrix, 0.0), axis=0, keepdims=True),
            (8, order),
        )
        diag_other = lane_partner(diagonal)
        diag_p = jnp.where(lane_lead, diagonal, diag_other)
        diag_q = jnp.where(lane_lead, diag_other, diagonal)
        cross = jnp.where(lane_lead, lane_partner(cross_tail), cross_tail)
        diag_gap = diag_q - diag_p
        diag_sum = diag_p + diag_q
        rot_angle = 0.5 * jnp.arctan2(
            2.0 * cross * diag_gap, diag_gap * diag_gap + damping_ratio * diag_sum * diag_sum
        )
        cosine = jnp.cos(rot_angle)
        sine_val = jnp.sin(rot_angle)
        signed_sine = jnp.where(lane_lead, -sine_val, sine_val)
        cos_lane = jnp.broadcast_to(cosine[:1], (order, order))
        sin_lane = jnp.broadcast_to(signed_sine[:1], (order, order))
        cos_row = jnp.sum(jnp.where(identity, cos_lane, 0.0), axis=1, keepdims=True)
        sin_row = jnp.sum(jnp.where(identity, sin_lane, 0.0), axis=1, keepdims=True)
        gram_matrix = cos_lane * gram_matrix + sin_lane * lane_partner(gram_matrix)
        gram_matrix = cos_row * gram_matrix + sin_row * row_partner(gram_matrix)
        accum = cos_lane * accum + sin_lane * lane_partner(accum)
    q_ref[...] = accum


def inner_solve(gram_matrix):
    return pl.pallas_call(
        solve_kernel,
        out_shape=jax.ShapeDtypeStruct(gram_matrix.shape, gram_matrix.dtype),
    )(gram_matrix)


def relayout(tile_work):
    cycles, row_count, tile_count, tile_width = tile_work.shape
    split_view = tile_work.reshape(cycles, 1, row_count, tile_count, tile_width)
    received = lax.all_to_all(split_view, "row", split_axis=3, concat_axis=1, tiled=True)
    return received.reshape(cycles * received.shape[1] * row_count, tile_width)


def gather_kernel(src_ref, out_ref, gram_ref, land, send_sem, recv_sem, local_sem):
    cycles, height, tiles, width = src_ref.shape
    me_r = lax.axis_index("row")
    me_c = lax.axis_index("col")
    n_c = lax.axis_size("col")
    k_me = me_r * n_c + me_c

    barrier = pltpu.get_barrier_semaphore()
    for t in range(tiles):
        @pl.when(me_r != t)
        def _():
            pl.semaphore_signal(barrier, inc=1, device_id=(t, me_c), device_id_type=MESH)
    pl.semaphore_wait(barrier, tiles - 1)

    def rows_of(block):
        return land.at[pl.ds(pl.multiple_of(block * height, height), height)]

    sends = []
    for i in range(cycles):
        block = i * tiles + me_r
        local = pltpu.make_async_copy(src_ref.at[i, :, me_r, :], rows_of(block), local_sem.at[i])
        pl.when(block <= k_me)(local.start)
    for t in reversed(range(tiles)):
        for i in range(cycles):
            block = i * tiles + me_r
            wanted = (block <= t * n_c + me_c) & (me_r != t)
            copy = pltpu.make_async_remote_copy(
                src_ref=src_ref.at[i, :, t, :],
                dst_ref=rows_of(block),
                send_sem=send_sem.at[t, i],
                recv_sem=recv_sem.at[me_r, i],
                device_id=(t, me_c),
                device_id_type=MESH,
            )
            pl.when(wanted)(copy.start)
            sends.append((wanted, copy))
    gram_ref[...] = jnp.zeros_like(gram_ref)
    for i in range(cycles):
        for r in range(tiles):
            block = i * tiles + r
            columns = slice(block * height, (block + 1) * height)
            incoming = pltpu.make_async_remote_copy(
                src_ref=src_ref.at[i, :, r, :],
                dst_ref=land.at[columns],
                send_sem=send_sem.at[r, i],
                recv_sem=recv_sem.at[r, i],
                device_id=(r, me_c),
                device_id_type=MESH,
            )
            local = pltpu.make_async_copy(src_ref.at[i, :, r, :], land.at[columns], local_sem.at[i])
            pl.when((block <= k_me) & (me_r != r))(incoming.wait_recv)
            pl.when((block <= k_me) & (me_r == r))(local.wait)

            @pl.when(block <= k_me)
            def _():
                rows_in = land[columns, :]
                lines_in = rows_in.T
                out_ref[:, columns] = lines_in
                gram_ref[...] += jnp.dot(
                    lines_in, rows_in, precision=highest, preferred_element_type=jnp.float32
                )

            @pl.when(block > k_me)
            def _():
                out_ref[:, columns] = jnp.zeros((width, height), out_ref.dtype)

    for wanted, copy in sends:
        pl.when(wanted)(copy.wait_send)


def gather_columns(factor_tiles):
    cycles, height, tiles, width = factor_tiles.shape
    return pl.pallas_call(
        gather_kernel,
        out_shape=(
            jax.ShapeDtypeStruct((width, cycles * tiles * height), factor_tiles.dtype),
            jax.ShapeDtypeStruct((width, width), factor_tiles.dtype),
        ),
        in_specs=[pl.BlockSpec(memory_space=pl.ANY)],
        out_specs=(
            pl.BlockSpec(memory_space=pltpu.VMEM),
            pl.BlockSpec(memory_space=pltpu.VMEM),
        ),
        scratch_shapes=[
            pltpu.VMEM((cycles * tiles * height, width), factor_tiles.dtype),
            pltpu.SemaphoreType.DMA((tiles, cycles)),
            pltpu.SemaphoreType.DMA((tiles, cycles)),
            pltpu.SemaphoreType.DMA((cycles,)),
        ],
        compiler_params=pltpu.CompilerParams(
            collective_id=0, has_side_effects=True, vmem_limit_bytes=48 * 1024 * 1024
        ),
    )(factor_tiles)


def summed(parts):
    total = parts[0]
    for part in parts[1:]:
        total = total + part
    return total


def per_device(factor_tiles):
    half_width = factor_tiles.shape[-1] // 2
    column_lines, gram_matrix = gather_columns(factor_tiles)
    rows = column_lines.shape[1]
    span = rows // CHUNKS
    position = lax.axis_index(("row", "col"))
    devices_total = lax.axis_size(("row", "col"))
    first = position == 0
    last = position == devices_total - 1
    pieces = [column_lines[:, j * span:(j + 1) * span] for j in range(CHUNKS)]
    rotation = inner_solve(gram_matrix)
    lines = [jnp.einsum("in,ij->jn", piece, rotation, precision=highest) for piece in pieces]
    for round_index in range(1, OUTER):
        fresh = []
        for piece in lines:
            top_half = piece[:half_width]
            bottom_half = piece[half_width:]
            outgoing = jnp.where(first, bottom_half, top_half)
            arrived = passed_along(outgoing, ("row", "col"), 1)
            behind = passed_along(bottom_half, ("row", "col"), -1)
            new_top = jnp.where(first, top_half, arrived)
            new_bottom = jnp.where(last, top_half, behind)
            fresh.append(jnp.concatenate([new_top, new_bottom], axis=0))
        gram_matrix = summed(
            [jnp.einsum("in,jn->ij", piece, piece, precision=highest) for piece in fresh]
        )
        rotation = inner_solve(gram_matrix)
        if round_index + 1 < OUTER:
            lines = [jnp.einsum("in,ij->jn", piece, rotation, precision=highest) for piece in fresh]
        else:
            whole = jnp.concatenate(fresh, axis=1)
            return jnp.einsum("in,ij->nj", whole, rotation, precision=highest)


def solution(mesh):
    return jax.shard_map(
        per_device,
        mesh=mesh,
        in_specs=(P(None, "row", None, "col"),),
        out_specs=P(None, ("row", "col")),
        check_vma=False,
    )
```

```python
import jax
import jax.numpy as jnp
from jax import lax
from jax.sharding import PartitionSpec as P
from jax.experimental import pallas as pl
from jax.experimental.pallas import tpu as pltpu

MESH = pl.DeviceIdType.MESH

LOGB = 7
OUTER = 4
INNER = 8
CHUNKS = 2


damping_ratio = 0.01
highest = lax.Precision.HIGHEST


def passed_along(value, axis, steps):
    count = lax.axis_size(axis)
    leading, last = (max(0, -steps), min(count, count - steps))
    return lax.ppermute(value, axis, [(source, source + steps) for source in range(leading, last)])


def solve_kernel(g_ref, q_ref):
    order = g_ref.shape[0]
    gram_matrix = g_ref[...]
    rows = lax.broadcasted_iota(jnp.int32, (order, order), 0)
    cols = lax.broadcasted_iota(jnp.int32, (order, order), 1)
    identity = rows == cols
    accum = jnp.where(identity, 1.0, 0.0).astype(gram_matrix.dtype)
    lane_ids = lax.broadcasted_iota(jnp.int32, (8, order), 1)
    for inner_step in range(INNER):
        stride = 2 ** ((LOGB - 1 - inner_step) % LOGB)

        def lane_partner(value):
            lead = (lax.broadcasted_iota(jnp.int32, value.shape, 1) & stride) == 0
            ahead = pltpu.roll(value, order - stride, 1)
            behind = pltpu.roll(value, stride, 1)
            return jnp.where(lead, ahead, behind)

        def row_partner(value):
            lead = (lax.broadcasted_iota(jnp.int32, value.shape, 0) & stride) == 0
            ahead = pltpu.roll(value, order - stride, 0)
            behind = pltpu.roll(value, stride, 0)
            return jnp.where(lead, ahead, behind)

        lane_lead = (lane_ids & stride) == 0
        diagonal = jnp.broadcast_to(
            jnp.sum(jnp.where(identity, gram_matrix, 0.0), axis=0, keepdims=True), (8, order)
        )
        cross_tail = jnp.broadcast_to(
            jnp.sum(jnp.where(rows == (cols ^ stride), gram_matrix, 0.0), axis=0, keepdims=True),
            (8, order),
        )
        diag_other = lane_partner(diagonal)
        diag_p = jnp.where(lane_lead, diagonal, diag_other)
        diag_q = jnp.where(lane_lead, diag_other, diagonal)
        cross = jnp.where(lane_lead, lane_partner(cross_tail), cross_tail)
        diag_gap = diag_q - diag_p
        diag_sum = diag_p + diag_q
        rot_angle = 0.5 * jnp.arctan2(
            2.0 * cross * diag_gap, diag_gap * diag_gap + damping_ratio * diag_sum * diag_sum
        )
        cosine = jnp.cos(rot_angle)
        sine_val = jnp.sin(rot_angle)
        signed_sine = jnp.where(lane_lead, -sine_val, sine_val)
        cos_lane = jnp.broadcast_to(cosine[:1], (order, order))
        sin_lane = jnp.broadcast_to(signed_sine[:1], (order, order))
        cos_row = jnp.sum(jnp.where(identity, cos_lane, 0.0), axis=1, keepdims=True)
        sin_row = jnp.sum(jnp.where(identity, sin_lane, 0.0), axis=1, keepdims=True)
        gram_matrix = cos_lane * gram_matrix + sin_lane * lane_partner(gram_matrix)
        gram_matrix = cos_row * gram_matrix + sin_row * row_partner(gram_matrix)
        accum = cos_lane * accum + sin_lane * lane_partner(accum)
    q_ref[...] = accum


def inner_solve(gram_matrix):
    return pl.pallas_call(
        solve_kernel,
        out_shape=jax.ShapeDtypeStruct(gram_matrix.shape, gram_matrix.dtype),
    )(gram_matrix)


def relayout(tile_work):
    cycles, row_count, tile_count, tile_width = tile_work.shape
    split_view = tile_work.reshape(cycles, 1, row_count, tile_count, tile_width)
    received = lax.all_to_all(split_view, "row", split_axis=3, concat_axis=1, tiled=True)
    return received.reshape(cycles * received.shape[1] * row_count, tile_width)


def gather_kernel(src_ref, out_ref, gram_ref, land, send_sem, recv_sem, local_sem):
    cycles, height, tiles, width = src_ref.shape
    me_r = lax.axis_index("row")
    me_c = lax.axis_index("col")
    n_c = lax.axis_size("col")
    k_me = me_r * n_c + me_c

    barrier = pltpu.get_barrier_semaphore()
    for t in range(tiles):
        @pl.when(me_r != t)
        def _():
            pl.semaphore_signal(barrier, inc=1, device_id=(t, me_c), device_id_type=MESH)
    pl.semaphore_wait(barrier, tiles - 1)

    def rows_of(block):
        return land.at[pl.ds(pl.multiple_of(block * height, height), height)]

    sends = []
    for i in range(cycles):
        block = i * tiles + me_r
        local = pltpu.make_async_copy(src_ref.at[i, :, me_r, :], rows_of(block), local_sem.at[i])
        pl.when(block <= k_me)(local.start)
        for t in range(tiles):
            wanted = (block <= t * n_c + me_c) & (me_r != t)
            copy = pltpu.make_async_remote_copy(
                src_ref=src_ref.at[i, :, t, :],
                dst_ref=rows_of(block),
                send_sem=send_sem.at[t, i],
                recv_sem=recv_sem.at[me_r, i],
                device_id=(t, me_c),
                device_id_type=MESH,
            )
            pl.when(wanted)(copy.start)
            sends.append((wanted, copy))
    gram_ref[...] = jnp.zeros_like(gram_ref)
    for i in range(cycles):
        for r in range(tiles):
            block = i * tiles + r
            columns = slice(block * height, (block + 1) * height)
            incoming = pltpu.make_async_remote_copy(
                src_ref=src_ref.at[i, :, r, :],
                dst_ref=land.at[columns],
                send_sem=send_sem.at[r, i],
                recv_sem=recv_sem.at[r, i],
                device_id=(r, me_c),
                device_id_type=MESH,
            )
            local = pltpu.make_async_copy(src_ref.at[i, :, r, :], land.at[columns], local_sem.at[i])
            pl.when((block <= k_me) & (me_r != r))(incoming.wait_recv)
            pl.when((block <= k_me) & (me_r == r))(local.wait)

            @pl.when(block <= k_me)
            def _():
                rows_in = land[columns, :]
                lines_in = rows_in.T
                out_ref[:, columns] = lines_in
                gram_ref[...] += jnp.dot(
                    lines_in, rows_in, precision=highest, preferred_element_type=jnp.float32
                )

            @pl.when(block > k_me)
            def _():
                out_ref[:, columns] = jnp.zeros((width, height), out_ref.dtype)

    for wanted, copy in sends:
        pl.when(wanted)(copy.wait_send)


def gather_columns(factor_tiles):
    cycles, height, tiles, width = factor_tiles.shape
    return pl.pallas_call(
        gather_kernel,
        out_shape=(
            jax.ShapeDtypeStruct((width, cycles * tiles * height), factor_tiles.dtype),
            jax.ShapeDtypeStruct((width, width), factor_tiles.dtype),
        ),
        in_specs=[pl.BlockSpec(memory_space=pl.ANY)],
        out_specs=(
            pl.BlockSpec(memory_space=pltpu.VMEM),
            pl.BlockSpec(memory_space=pltpu.VMEM),
        ),
        scratch_shapes=[
            pltpu.VMEM((cycles * tiles * height, width), factor_tiles.dtype),
            pltpu.SemaphoreType.DMA((tiles, cycles)),
            pltpu.SemaphoreType.DMA((tiles, cycles)),
            pltpu.SemaphoreType.DMA((cycles,)),
        ],
        compiler_params=pltpu.CompilerParams(
            collective_id=0, has_side_effects=True, vmem_limit_bytes=48 * 1024 * 1024
        ),
    )(factor_tiles)


def summed(parts):
    total = parts[0]
    for part in parts[1:]:
        total = total + part
    return total


def per_device(factor_tiles):
    half_width = factor_tiles.shape[-1] // 2
    column_lines, gram_matrix = gather_columns(factor_tiles)
    rows = column_lines.shape[1]
    span = rows // CHUNKS
    position = lax.axis_index(("row", "col"))
    devices_total = lax.axis_size(("row", "col"))
    first = position == 0
    last = position == devices_total - 1
    pieces = [column_lines[:, j * span:(j + 1) * span] for j in range(CHUNKS)]

    def halves(piece, rotation):
        top_cols = rotation[:, :half_width]
        bottom_cols = rotation[:, half_width:]
        sent_cols = jnp.where(first, bottom_cols, top_cols)
        kept_cols = jnp.where(first, top_cols, bottom_cols)
        sent = jnp.einsum("in,ij->jn", piece, sent_cols, precision=highest)
        kept = jnp.einsum("in,ij->jn", piece, kept_cols, precision=highest)
        return sent, kept

    rotation = inner_solve(gram_matrix)
    lines = [halves(piece, rotation) for piece in pieces]
    for round_index in range(1, OUTER):
        fresh = []
        for outgoing, kept in lines:
            arrived = passed_along(outgoing, ("row", "col"), 1)
            behind = passed_along(kept, ("row", "col"), -1)
            new_top = jnp.where(first, kept, arrived)
            new_bottom = jnp.where(last, outgoing, behind)
            fresh.append(jnp.concatenate([new_top, new_bottom], axis=0))
        gram_matrix = summed(
            [jnp.einsum("in,jn->ij", piece, piece, precision=highest) for piece in fresh]
        )
        rotation = inner_solve(gram_matrix)
        if round_index + 1 < OUTER:
            lines = [halves(piece, rotation) for piece in fresh]
        else:
            whole = jnp.concatenate(fresh, axis=1)
            return jnp.einsum("in,ij->nj", whole, rotation, precision=highest)


def solution(mesh):
    return jax.shard_map(
        per_device,
        mesh=mesh,
        in_specs=(P(None, "row", None, "col"),),
        out_specs=P(None, ("row", "col")),
        check_vma=False,
    )
```

```python
import jax
import jax.numpy as jnp
from jax import lax
from jax.sharding import PartitionSpec as P
from jax.experimental import pallas as pl
from jax.experimental.pallas import tpu as pltpu

MESH = pl.DeviceIdType.MESH

LOGB = 7
OUTER = 4
INNER = 8
CHUNKS = 2


damping_ratio = 0.01
highest = lax.Precision.HIGHEST


def passed_along(value, axis, steps):
    count = lax.axis_size(axis)
    leading, last = (max(0, -steps), min(count, count - steps))
    return lax.ppermute(value, axis, [(source, source + steps) for source in range(leading, last)])


def solve_kernel(g_ref, q_ref):
    order = g_ref.shape[0]
    gram_matrix = g_ref[...]
    rows = lax.broadcasted_iota(jnp.int32, (order, order), 0)
    cols = lax.broadcasted_iota(jnp.int32, (order, order), 1)
    identity = rows == cols
    accum = jnp.where(identity, 1.0, 0.0).astype(gram_matrix.dtype)
    lane_ids = lax.broadcasted_iota(jnp.int32, (8, order), 1)
    for inner_step in range(INNER):
        stride = 2 ** ((LOGB - 1 - inner_step) % LOGB)

        def lane_partner(value):
            lead = (lax.broadcasted_iota(jnp.int32, value.shape, 1) & stride) == 0
            ahead = pltpu.roll(value, order - stride, 1)
            behind = pltpu.roll(value, stride, 1)
            return jnp.where(lead, ahead, behind)

        def row_partner(value):
            lead = (lax.broadcasted_iota(jnp.int32, value.shape, 0) & stride) == 0
            ahead = pltpu.roll(value, order - stride, 0)
            behind = pltpu.roll(value, stride, 0)
            return jnp.where(lead, ahead, behind)

        lane_lead = (lane_ids & stride) == 0
        diagonal = jnp.broadcast_to(
            jnp.sum(jnp.where(identity, gram_matrix, 0.0), axis=0, keepdims=True), (8, order)
        )
        cross_tail = jnp.broadcast_to(
            jnp.sum(jnp.where(rows == (cols ^ stride), gram_matrix, 0.0), axis=0, keepdims=True),
            (8, order),
        )
        diag_other = lane_partner(diagonal)
        diag_p = jnp.where(lane_lead, diagonal, diag_other)
        diag_q = jnp.where(lane_lead, diag_other, diagonal)
        cross = jnp.where(lane_lead, lane_partner(cross_tail), cross_tail)
        diag_gap = diag_q - diag_p
        diag_sum = diag_p + diag_q
        rot_angle = 0.5 * jnp.arctan2(
            2.0 * cross * diag_gap, diag_gap * diag_gap + damping_ratio * diag_sum * diag_sum
        )
        cosine = jnp.cos(rot_angle)
        sine_val = jnp.sin(rot_angle)
        signed_sine = jnp.where(lane_lead, -sine_val, sine_val)
        cos_lane = jnp.broadcast_to(cosine[:1], (order, order))
        sin_lane = jnp.broadcast_to(signed_sine[:1], (order, order))
        cos_row = jnp.sum(jnp.where(identity, cos_lane, 0.0), axis=1, keepdims=True)
        sin_row = jnp.sum(jnp.where(identity, sin_lane, 0.0), axis=1, keepdims=True)
        gram_matrix = cos_lane * gram_matrix + sin_lane * lane_partner(gram_matrix)
        gram_matrix = cos_row * gram_matrix + sin_row * row_partner(gram_matrix)
        accum = cos_lane * accum + sin_lane * lane_partner(accum)
    q_ref[...] = accum


def inner_solve(gram_matrix):
    return pl.pallas_call(
        solve_kernel,
        out_shape=jax.ShapeDtypeStruct(gram_matrix.shape, gram_matrix.dtype),
    )(gram_matrix)


def relayout(tile_work):
    cycles, row_count, tile_count, tile_width = tile_work.shape
    split_view = tile_work.reshape(cycles, 1, row_count, tile_count, tile_width)
    received = lax.all_to_all(split_view, "row", split_axis=3, concat_axis=1, tiled=True)
    return received.reshape(cycles * received.shape[1] * row_count, tile_width)


def gather_kernel(src_ref, out_ref, gram_ref, land, send_sem, recv_sem, local_sem):
    cycles, height, tiles, width = src_ref.shape
    me_r = lax.axis_index("row")
    me_c = lax.axis_index("col")
    n_c = lax.axis_size("col")
    k_me = me_r * n_c + me_c

    barrier = pltpu.get_barrier_semaphore()
    for t in range(tiles):
        @pl.when(me_r != t)
        def _():
            pl.semaphore_signal(barrier, inc=1, device_id=(t, me_c), device_id_type=MESH)
    pl.semaphore_wait(barrier, tiles - 1)

    def rows_of(block):
        return land.at[pl.ds(pl.multiple_of(block * height, height), height)]

    sends = []
    for i in range(cycles):
        block = i * tiles + me_r
        local = pltpu.make_async_copy(src_ref.at[i, :, me_r, :], rows_of(block), local_sem.at[i])
        pl.when(block <= k_me)(local.start)
        for t in reversed(range(tiles)):
            wanted = (block <= t * n_c + me_c) & (me_r != t)
            copy = pltpu.make_async_remote_copy(
                src_ref=src_ref.at[i, :, t, :],
                dst_ref=rows_of(block),
                send_sem=send_sem.at[t, i],
                recv_sem=recv_sem.at[me_r, i],
                device_id=(t, me_c),
                device_id_type=MESH,
            )
            pl.when(wanted)(copy.start)
            sends.append((wanted, copy))
    gram_ref[...] = jnp.zeros_like(gram_ref)
    for i in range(cycles):
        for r in range(tiles):
            block = i * tiles + r
            columns = slice(block * height, (block + 1) * height)
            incoming = pltpu.make_async_remote_copy(
                src_ref=src_ref.at[i, :, r, :],
                dst_ref=land.at[columns],
                send_sem=send_sem.at[r, i],
                recv_sem=recv_sem.at[r, i],
                device_id=(r, me_c),
                device_id_type=MESH,
            )
            local = pltpu.make_async_copy(src_ref.at[i, :, r, :], land.at[columns], local_sem.at[i])
            pl.when((block <= k_me) & (me_r != r))(incoming.wait_recv)
            pl.when((block <= k_me) & (me_r == r))(local.wait)

            @pl.when(block <= k_me)
            def _():
                rows_in = land[columns, :]
                lines_in = rows_in.T
                out_ref[:, columns] = lines_in
                gram_ref[...] += jnp.dot(
                    lines_in, rows_in, precision=highest, preferred_element_type=jnp.float32
                )

            @pl.when(block > k_me)
            def _():
                out_ref[:, columns] = jnp.zeros((width, height), out_ref.dtype)

    for wanted, copy in sends:
        pl.when(wanted)(copy.wait_send)


def gather_columns(factor_tiles):
    cycles, height, tiles, width = factor_tiles.shape
    return pl.pallas_call(
        gather_kernel,
        out_shape=(
            jax.ShapeDtypeStruct((width, cycles * tiles * height), factor_tiles.dtype),
            jax.ShapeDtypeStruct((width, width), factor_tiles.dtype),
        ),
        in_specs=[pl.BlockSpec(memory_space=pl.ANY)],
        out_specs=(
            pl.BlockSpec(memory_space=pltpu.VMEM),
            pl.BlockSpec(memory_space=pltpu.VMEM),
        ),
        scratch_shapes=[
            pltpu.VMEM((cycles * tiles * height, width), factor_tiles.dtype),
            pltpu.SemaphoreType.DMA((tiles, cycles)),
            pltpu.SemaphoreType.DMA((tiles, cycles)),
            pltpu.SemaphoreType.DMA((cycles,)),
        ],
        compiler_params=pltpu.CompilerParams(
            collective_id=0, has_side_effects=True, vmem_limit_bytes=48 * 1024 * 1024
        ),
    )(factor_tiles)


def summed(parts):
    total = parts[0]
    for part in parts[1:]:
        total = total + part
    return total


def per_device(factor_tiles):
    half_width = factor_tiles.shape[-1] // 2
    column_lines, gram_matrix = gather_columns(factor_tiles)
    rows = column_lines.shape[1]
    span = rows // CHUNKS
    position = lax.axis_index(("row", "col"))
    devices_total = lax.axis_size(("row", "col"))
    first = position == 0
    last = position == devices_total - 1
    pieces = [column_lines[:, j * span:(j + 1) * span] for j in range(CHUNKS)]
    rotation = inner_solve(gram_matrix)
    lines = [jnp.einsum("in,ij->jn", piece, rotation, precision=highest) for piece in pieces]
    for round_index in range(1, OUTER):
        fresh = []
        for piece in lines:
            top_half = piece[:half_width]
            bottom_half = piece[half_width:]
            outgoing = jnp.where(first, bottom_half, top_half)
            arrived = passed_along(outgoing, ("row", "col"), 1)
            behind = passed_along(bottom_half, ("row", "col"), -1)
            new_top = jnp.where(first, top_half, arrived)
            new_bottom = jnp.where(last, top_half, behind)
            fresh.append(jnp.concatenate([new_top, new_bottom], axis=0))
        gram_matrix = summed(
            [jnp.einsum("in,jn->ij", piece, piece, precision=highest) for piece in fresh]
        )
        rotation = inner_solve(gram_matrix)
        if round_index + 1 < OUTER:
            lines = [jnp.einsum("in,ij->jn", piece, rotation, precision=highest) for piece in fresh]
        else:
            whole = jnp.concatenate(fresh, axis=1)
            return jnp.einsum("in,ij->nj", whole, rotation, precision=highest)


def solution(mesh):
    return jax.shard_map(
        per_device,
        mesh=mesh,
        in_specs=(P(None, "row", None, "col"),),
        out_specs=P(None, ("row", "col")),
        check_vma=False,
    )
```

```python
import jax
import jax.numpy as jnp
from jax import lax
from jax.sharding import PartitionSpec as P
from jax.experimental import pallas as pl
from jax.experimental.pallas import tpu as pltpu

MESH = pl.DeviceIdType.MESH

LOGB = 7
OUTER = 4
INNER = 8
CHUNKS = 2


damping_ratio = 0.01
highest = lax.Precision.HIGHEST


def passed_along(value, axis, steps):
    count = lax.axis_size(axis)
    leading, last = (max(0, -steps), min(count, count - steps))
    return lax.ppermute(value, axis, [(source, source + steps) for source in range(leading, last)])


def solve_kernel(g_ref, q_ref):
    order = g_ref.shape[0]
    gram_matrix = g_ref[...]
    rows = lax.broadcasted_iota(jnp.int32, (order, order), 0)
    cols = lax.broadcasted_iota(jnp.int32, (order, order), 1)
    identity = rows == cols
    accum = jnp.where(identity, 1.0, 0.0).astype(gram_matrix.dtype)
    lane_ids = lax.broadcasted_iota(jnp.int32, (8, order), 1)
    for inner_step in range(INNER):
        stride = 2 ** ((LOGB - 1 - inner_step) % LOGB)

        def lane_partner(value):
            lead = (lax.broadcasted_iota(jnp.int32, value.shape, 1) & stride) == 0
            ahead = pltpu.roll(value, order - stride, 1)
            behind = pltpu.roll(value, stride, 1)
            return jnp.where(lead, ahead, behind)

        def row_partner(value):
            lead = (lax.broadcasted_iota(jnp.int32, value.shape, 0) & stride) == 0
            ahead = pltpu.roll(value, order - stride, 0)
            behind = pltpu.roll(value, stride, 0)
            return jnp.where(lead, ahead, behind)

        lane_lead = (lane_ids & stride) == 0
        diagonal = jnp.broadcast_to(
            jnp.sum(jnp.where(identity, gram_matrix, 0.0), axis=0, keepdims=True), (8, order)
        )
        cross_tail = jnp.broadcast_to(
            jnp.sum(jnp.where(rows == (cols ^ stride), gram_matrix, 0.0), axis=0, keepdims=True),
            (8, order),
        )
        diag_other = lane_partner(diagonal)
        diag_p = jnp.where(lane_lead, diagonal, diag_other)
        diag_q = jnp.where(lane_lead, diag_other, diagonal)
        cross = jnp.where(lane_lead, lane_partner(cross_tail), cross_tail)
        diag_gap = diag_q - diag_p
        diag_sum = diag_p + diag_q
        rot_angle = 0.5 * jnp.arctan2(
            2.0 * cross * diag_gap, diag_gap * diag_gap + damping_ratio * diag_sum * diag_sum
        )
        cosine = jnp.cos(rot_angle)
        sine_val = jnp.sin(rot_angle)
        signed_sine = jnp.where(lane_lead, -sine_val, sine_val)
        cos_lane = jnp.broadcast_to(cosine[:1], (order, order))
        sin_lane = jnp.broadcast_to(signed_sine[:1], (order, order))
        cos_row = jnp.transpose(cosine)[:, :1]
        sin_row = jnp.transpose(signed_sine)[:, :1]
        gram_matrix = cos_lane * gram_matrix + sin_lane * lane_partner(gram_matrix)
        gram_matrix = cos_row * gram_matrix + sin_row * row_partner(gram_matrix)
        accum = cos_lane * accum + sin_lane * lane_partner(accum)
    q_ref[...] = accum


def inner_solve(gram_matrix):
    return pl.pallas_call(
        solve_kernel,
        out_shape=jax.ShapeDtypeStruct(gram_matrix.shape, gram_matrix.dtype),
    )(gram_matrix)


def relayout(tile_work):
    cycles, row_count, tile_count, tile_width = tile_work.shape
    split_view = tile_work.reshape(cycles, 1, row_count, tile_count, tile_width)
    received = lax.all_to_all(split_view, "row", split_axis=3, concat_axis=1, tiled=True)
    return received.reshape(cycles * received.shape[1] * row_count, tile_width)


def gather_kernel(src_ref, out_ref, gram_ref, land, send_sem, recv_sem, local_sem):
    cycles, height, tiles, width = src_ref.shape
    me_r = lax.axis_index("row")
    me_c = lax.axis_index("col")
    n_c = lax.axis_size("col")
    k_me = me_r * n_c + me_c

    barrier = pltpu.get_barrier_semaphore()
    for t in range(tiles):
        @pl.when(me_r != t)
        def _():
            pl.semaphore_signal(barrier, inc=1, device_id=(t, me_c), device_id_type=MESH)
    pl.semaphore_wait(barrier, tiles - 1)

    def rows_of(block):
        return land.at[pl.ds(pl.multiple_of(block * height, height), height)]

    sends = []
    for i in range(cycles):
        block = i * tiles + me_r
        local = pltpu.make_async_copy(src_ref.at[i, :, me_r, :], rows_of(block), local_sem.at[i])
        pl.when(block <= k_me)(local.start)
        for t in range(tiles):
            wanted = (block <= t * n_c + me_c) & (me_r != t)
            copy = pltpu.make_async_remote_copy(
                src_ref=src_ref.at[i, :, t, :],
                dst_ref=rows_of(block),
                send_sem=send_sem.at[t, i],
                recv_sem=recv_sem.at[me_r, i],
                device_id=(t, me_c),
                device_id_type=MESH,
            )
            pl.when(wanted)(copy.start)
            sends.append((wanted, copy))
    gram_ref[...] = jnp.zeros_like(gram_ref)
    for i in range(cycles):
        for r in range(tiles):
            block = i * tiles + r
            columns = slice(block * height, (block + 1) * height)
            incoming = pltpu.make_async_remote_copy(
                src_ref=src_ref.at[i, :, r, :],
                dst_ref=land.at[columns],
                send_sem=send_sem.at[r, i],
                recv_sem=recv_sem.at[r, i],
                device_id=(r, me_c),
                device_id_type=MESH,
            )
            local = pltpu.make_async_copy(src_ref.at[i, :, r, :], land.at[columns], local_sem.at[i])
            pl.when((block <= k_me) & (me_r != r))(incoming.wait_recv)
            pl.when((block <= k_me) & (me_r == r))(local.wait)

            @pl.when(block <= k_me)
            def _():
                rows_in = land[columns, :]
                lines_in = rows_in.T
                out_ref[:, columns] = lines_in
                gram_ref[...] += jnp.dot(
                    lines_in, rows_in, precision=highest, preferred_element_type=jnp.float32
                )

            @pl.when(block > k_me)
            def _():
                out_ref[:, columns] = jnp.zeros((width, height), out_ref.dtype)

    for wanted, copy in sends:
        pl.when(wanted)(copy.wait_send)


def gather_columns(factor_tiles):
    cycles, height, tiles, width = factor_tiles.shape
    return pl.pallas_call(
        gather_kernel,
        out_shape=(
            jax.ShapeDtypeStruct((width, cycles * tiles * height), factor_tiles.dtype),
            jax.ShapeDtypeStruct((width, width), factor_tiles.dtype),
        ),
        in_specs=[pl.BlockSpec(memory_space=pl.ANY)],
        out_specs=(
            pl.BlockSpec(memory_space=pltpu.VMEM),
            pl.BlockSpec(memory_space=pltpu.VMEM),
        ),
        scratch_shapes=[
            pltpu.VMEM((cycles * tiles * height, width), factor_tiles.dtype),
            pltpu.SemaphoreType.DMA((tiles, cycles)),
            pltpu.SemaphoreType.DMA((tiles, cycles)),
            pltpu.SemaphoreType.DMA((cycles,)),
        ],
        compiler_params=pltpu.CompilerParams(
            collective_id=0, has_side_effects=True, vmem_limit_bytes=48 * 1024 * 1024
        ),
    )(factor_tiles)


def summed(parts):
    total = parts[0]
    for part in parts[1:]:
        total = total + part
    return total


def per_device(factor_tiles):
    half_width = factor_tiles.shape[-1] // 2
    column_lines, gram_matrix = gather_columns(factor_tiles)
    rows = column_lines.shape[1]
    span = rows // CHUNKS
    position = lax.axis_index(("row", "col"))
    devices_total = lax.axis_size(("row", "col"))
    first = position == 0
    last = position == devices_total - 1
    pieces = [column_lines[:, j * span:(j + 1) * span] for j in range(CHUNKS)]
    rotation = inner_solve(gram_matrix)
    lines = [jnp.einsum("in,ij->jn", piece, rotation, precision=highest) for piece in pieces]
    for round_index in range(1, OUTER):
        fresh = []
        for piece in lines:
            top_half = piece[:half_width]
            bottom_half = piece[half_width:]
            outgoing = jnp.where(first, bottom_half, top_half)
            arrived = passed_along(outgoing, ("row", "col"), 1)
            behind = passed_along(bottom_half, ("row", "col"), -1)
            new_top = jnp.where(first, top_half, arrived)
            new_bottom = jnp.where(last, top_half, behind)
            fresh.append(jnp.concatenate([new_top, new_bottom], axis=0))
        gram_matrix = summed(
            [jnp.einsum("in,jn->ij", piece, piece, precision=highest) for piece in fresh]
        )
        rotation = inner_solve(gram_matrix)
        if round_index + 1 < OUTER:
            lines = [jnp.einsum("in,ij->jn", piece, rotation, precision=highest) for piece in fresh]
        else:
            whole = jnp.concatenate(fresh, axis=1)
            return jnp.einsum("in,ij->nj", whole, rotation, precision=highest)


def solution(mesh):
    return jax.shard_map(
        per_device,
        mesh=mesh,
        in_specs=(P(None, "row", None, "col"),),
        out_specs=P(None, ("row", "col")),
        check_vma=False,
    )
```
